128 devices in a mesh: dp: 8 (over y, z_lo), ctx: 16 (over z_hi, x, core).
Axes of the slice: x: 4, y: 4, z: 4 (z_hi: 2, z_lo: 2; z = z_hi * 2 + z_lo), core: 2. Of those that a mesh axis runs over, the one named last changes fastest.
Arguments:
- hidden_in: bfloat16 [8, 2048, 4096], P('dp', 'ctx'), may hold values from -6 to 6
- write_weight: bfloat16 [4096, 128], P(('dp', 'ctx')), may hold values from -0.09375 to 0.09375
- shard_scale: float32 [128], P(('dp', 'ctx')), may hold values from 0.5 to 2
- inner_acts: bfloat16 [8, 2048, 4096], P('dp', 'ctx'), may hold values from -6 to 6
- read_proj: bfloat16 [8, 2048, 128], P('dp', 'ctx'), may hold values from -0.13183594 to 0.13183594
- step_size: float32 [8, 64, 2048], P('dp', None, 'ctx'), may hold values from 0.1 to 1
- log_decay: float32 [8, 64, 2048], P('dp', None, 'ctx'), may hold values from -2 to 0
- grad_fwd: bfloat16 [8, 2048, 4096], P('dp', 'ctx'), may hold values from -1.5 to 1.5
- grad_rev: bfloat16 [8, 2048, 4096], P('dp', 'ctx'), may hold values from -1.5 to 1.5
Outputs:
- grad_inner: bfloat16 [8, 2048, 4096], P('dp', 'ctx')
- grad_hidden: bfloat16 [8, 2048, 4096], P('dp', 'ctx')
- grad_weight: float32 [4096, 128], P(('dp', 'ctx'))
The draws below stay inside these ranges and needn't reach their ends.
All inputs are finite; a program needn't handle non-finite values.
Results may differ from the reference program's by a relative error of at most 0.0064.
Values may be sent and summed in bfloat16 or wider, within the bound.
A program may use at most 256 MiB of HBM per device.

```python
import math
import jax
import jax.numpy as jnp
from jax import lax

D = 4096
HALF_HEADS = 64
STATE = 128
BLOCK = 128
TOK_DEV = 128
E = 4096
SEQUENCE_LENGTH = 2048
BATCH_SEQUENCES = 8
SHARDS = 128


def draw_log_decay(key, part):
    random_subkeys = jax.random.split(key, 5)
    fast_limit = 4
    fast_heads = jax.random.randint(random_subkeys[0], (BATCH_SEQUENCES, HALF_HEADS, 1), 0, 8) < fast_limit
    baseline_rate = jnp.where(fast_heads, 0.08, 0.3 / SEQUENCE_LENGTH)
    jaggedness = jnp.exp(jax.random.uniform(random_subkeys[1], (BATCH_SEQUENCES, HALF_HEADS, SEQUENCE_LENGTH), minval=-0.7, maxval=0.7))
    span_count = SEQUENCE_LENGTH // TOK_DEV
    block_factor_scale = jnp.exp(jax.random.uniform(random_subkeys[2], (BATCH_SEQUENCES, HALF_HEADS, span_count, 1), minval=-0.7, maxval=0.7))
    block_factor_scale = jnp.broadcast_to(block_factor_scale, (BATCH_SEQUENCES, HALF_HEADS, span_count, TOK_DEV)).reshape(BATCH_SEQUENCES, HALF_HEADS, SEQUENCE_LENGTH)
    spike_locations = jax.random.randint(random_subkeys[3], (BATCH_SEQUENCES, HALF_HEADS, 2, 1), 0, SEQUENCE_LENGTH)
    spike_decrements = jnp.log(jax.random.uniform(random_subkeys[4], (BATCH_SEQUENCES, HALF_HEADS, 2, 1), minval=0.5, maxval=0.8))
    position_indices = jnp.arange(SEQUENCE_LENGTH)[None, None, None, :]
    spike_events = jnp.sum(jnp.where(position_indices == spike_locations, spike_decrements, 0.0), axis=2)
    return (-baseline_rate * jaggedness * block_factor_scale + spike_events).astype(jnp.float32)


def block_levels(rng, extent, cuts, least, largest):
    level, own = 1.0, jax.random.fold_in(rng, 6)
    for position, blocks in cuts:
        steps = jnp.exp(jax.random.uniform(jax.random.fold_in(own, position), (blocks,), jnp.float32, least / len(cuts), largest / len(cuts)))
        level = level * jnp.repeat(steps, extent[position] // blocks).reshape([-1 if axis == position else 1 for axis in range(len(extent))])
    return level


def noise(key, shape, spread, most, cuts=(), held_as=jnp.bfloat16):
    drawn = spread * jax.random.normal(key, shape, jnp.float32)
    if cuts:
        drawn = drawn * block_levels(key, shape, cuts, -0.22, 0.18)
    return jnp.clip(drawn, -most, most).astype(held_as)


def setup_inputs(seed: int = 0) -> dict:
    arg_keys = jax.random.split(jax.random.key(seed), 10)
    return {
        "hidden_in": noise(arg_keys[0], (BATCH_SEQUENCES, SEQUENCE_LENGTH, D), 1.0, 6.0, ((0, 8), (1, 16))),
        "write_weight": noise(arg_keys[1], (D, STATE), D ** -0.5, 0.09375, ((0, 128),)),
        "shard_scale": jnp.clip(jnp.exp(math.log(2.0) - 1.3862944 * jax.random.uniform(arg_keys[2], (SHARDS,), jnp.float32) ** block_levels(arg_keys[2], (SHARDS,), ((0, 128),), -0.2, 0.2)), 0.5, 2.0),
        "inner_acts": noise(arg_keys[3], (BATCH_SEQUENCES, SEQUENCE_LENGTH, E), 1.0, 6.0, ((0, 8), (1, 16))),
        "read_proj": noise(arg_keys[4], (BATCH_SEQUENCES, SEQUENCE_LENGTH, STATE), (0.25 / STATE ** 0.5), 0.13183594, ((0, 8), (1, 16))),
        "step_size": jnp.clip(jnp.exp(math.log(1.0) - 2.3025851 * jax.random.uniform(arg_keys[5], (BATCH_SEQUENCES, HALF_HEADS, SEQUENCE_LENGTH), jnp.float32) ** block_levels(arg_keys[5], (BATCH_SEQUENCES, HALF_HEADS, SEQUENCE_LENGTH), ((0, 8), (2, 16)), -0.2, 0.2)), 0.1, 1.0),
        "log_decay": draw_log_decay(jax.random.fold_in(arg_keys[9], 71), 0),
        "grad_fwd": noise(arg_keys[7], (BATCH_SEQUENCES, SEQUENCE_LENGTH, E), 0.25, 1.5, ((0, 8), (1, 16))),
        "grad_rev": noise(arg_keys[8], (BATCH_SEQUENCES, SEQUENCE_LENGTH, E), 0.25, 1.5, ((0, 8), (1, 16))),
    }


masked_low = -1e30


def decay_state(decays, state_mat):
    head_count = decays.shape[0]
    shaped = state_mat.reshape(state_mat.shape[0], head_count, state_mat.shape[1] // head_count)
    return (shaped * decays[None, :, None]).reshape(state_mat.shape)


def block_cums(decay_rows):
    local_cum = jnp.cumsum(decay_rows, axis=1)
    return local_cum, local_cum - decay_rows


def block_summary(read_rows, decay_rows, fwd_rows, back_rows):
    local_cum, local_excl = block_cums(decay_rows)
    block_end = local_cum[:, -1:]
    head_count = decay_rows.shape[0]
    row_count = fwd_rows.shape[0]
    col_count = fwd_rows.shape[1]
    fwd_weight = jnp.exp(local_cum).T
    back_weight = jnp.exp(block_end - local_excl).T
    fwd_scaled = (fwd_rows.astype(jnp.float32).reshape(row_count, head_count, col_count // head_count) * fwd_weight[:, :, None]).reshape(row_count, col_count).astype(jnp.bfloat16)
    back_scaled = (back_rows.astype(jnp.float32).reshape(row_count, head_count, col_count // head_count) * back_weight[:, :, None]).reshape(row_count, col_count).astype(jnp.bfloat16)
    right_part = jnp.dot(read_rows.T, fwd_scaled, preferred_element_type=jnp.float32)
    left_part = jnp.dot(read_rows.T, back_scaled, preferred_element_type=jnp.float32)
    return jnp.exp(block_end[:, 0]), right_part, left_part


def block_outputs(inner_rows, read_rows, write_rows, step_rows, decay_rows, fwd_rows, back_rows, right_in, left_in):
    local_cum, local_excl = block_cums(decay_rows)
    block_end = local_cum[:, -1:]
    row_count = inner_rows.shape[0]
    head_count = step_rows.shape[0]
    col_count = inner_rows.shape[1]
    head_dim = col_count // head_count
    kernel = jnp.dot(write_rows, read_rows.T, preferred_element_type=jnp.float32)
    position_indices = jnp.arange(row_count)
    upper_mask = position_indices[None, :] >= position_indices[:, None]
    lower_mask = position_indices[None, :] <= position_indices[:, None]
    fwd_decay = jnp.exp(jnp.where(upper_mask[None], local_cum[:, None, :] - local_cum[:, :, None], masked_low))
    rev_decay = jnp.exp(jnp.where(lower_mask[None], local_excl[:, :, None] - local_excl[:, None, :], masked_low))
    fwd_mix = (fwd_decay * kernel[None]).astype(jnp.bfloat16)
    rev_mix = (rev_decay * kernel[None]).astype(jnp.bfloat16)
    fwd_heads = fwd_rows.astype(jnp.float32).reshape(row_count, head_count, head_dim)
    back_heads = back_rows.astype(jnp.float32).reshape(row_count, head_count, head_dim)
    inner_heads = inner_rows.astype(jnp.float32).reshape(row_count, head_count, head_dim)
    intra_sum = jnp.einsum("hst,thp->shp", fwd_mix.astype(jnp.float32), fwd_heads) + jnp.einsum("hst,thp->shp", rev_mix.astype(jnp.float32), back_heads)
    write_float = write_rows.astype(jnp.float32)
    right_term = jnp.dot(write_float, right_in, precision=lax.Precision.HIGHEST).reshape(row_count, head_count, head_dim)
    left_term = jnp.dot(write_float, left_in, precision=lax.Precision.HIGHEST).reshape(row_count, head_count, head_dim)
    fwd_edge = jnp.exp(block_end - local_cum).T
    back_edge = jnp.exp(local_excl).T
    step_cols = step_rows.T
    combined = intra_sum + fwd_edge[:, :, None] * right_term + back_edge[:, :, None] * left_term
    grad_block = (step_cols[:, :, None] * combined).reshape(row_count, col_count).astype(jnp.bfloat16)
    fwd_dots = jnp.einsum("thp,shp->hst", fwd_heads, inner_heads)
    back_dots = jnp.einsum("thp,shp->hst", back_heads, inner_heads)
    mixed_weights = jnp.sum(step_rows[:, :, None] * (fwd_decay * fwd_dots + rev_decay * back_dots), axis=0).astype(jnp.bfloat16)
    intra_write = jnp.dot(mixed_weights, read_rows, preferred_element_type=jnp.float32)
    fwd_inner = (inner_heads * (step_cols * fwd_edge)[:, :, None]).reshape(row_count, col_count)
    back_inner = (inner_heads * (step_cols * back_edge)[:, :, None]).reshape(row_count, col_count)
    edge_write = jnp.dot(fwd_inner, right_in.T, precision=lax.Precision.HIGHEST) + jnp.dot(back_inner, left_in.T, precision=lax.Precision.HIGHEST)
    write_block = (intra_write + edge_write).astype(jnp.bfloat16)
    return grad_block, write_block


def reference(hidden_in, write_weight, shard_scale, inner_acts, read_proj, step_size, log_decay, grad_fwd, grad_rev):
    shard_rows = D // SHARDS
    weight_eff = (write_weight.astype(jnp.float32) * jnp.repeat(shard_scale, shard_rows)[:, None]).astype(jnp.bfloat16)
    block_count = SEQUENCE_LENGTH // BLOCK

    def split_rows(array):
        return array.reshape(block_count, BLOCK, array.shape[-1])

    def split_cols(array):
        return array.reshape(array.shape[0], block_count, BLOCK).transpose(1, 0, 2)

    def carry_step(state_mat, block_item):
        factor, part_state = block_item
        return part_state + decay_state(factor, state_mat), state_mat

    def one_sequence(accumulated, seq_item):
        hidden, inner_seq, read_seq, step_seq, decay_seq, fwd_seq, rev_seq = seq_item
        write_seq = jnp.dot(hidden, weight_eff, preferred_element_type=jnp.float32).astype(jnp.bfloat16)
        back_seq = rev_seq[::-1]
        read_blocks = split_rows(read_seq)
        decay_blocks = split_cols(decay_seq)
        fwd_blocks = split_rows(fwd_seq)
        back_blocks = split_rows(back_seq)
        decays, right_parts, left_parts = lax.map(lambda block_item: block_summary(*block_item), (read_blocks, decay_blocks, fwd_blocks, back_blocks))
        zero_state = jnp.zeros((STATE, E), jnp.float32)
        ignored, right_ins = lax.scan(carry_step, zero_state, (decays, right_parts), reverse=True)
        ignored, left_ins = lax.scan(carry_step, zero_state, (decays, left_parts))
        grad_blocks, write_blocks = lax.map(lambda block_item: block_outputs(*block_item), (split_rows(inner_seq), read_blocks, split_rows(write_seq), split_cols(step_seq), decay_blocks, fwd_blocks, back_blocks, right_ins, left_ins))
        grad_write = write_blocks.reshape(SEQUENCE_LENGTH, STATE)
        grad_hid = jnp.dot(grad_write, weight_eff.T, preferred_element_type=jnp.float32).astype(jnp.bfloat16)
        accumulated = accumulated + jnp.dot(hidden.T, grad_write, preferred_element_type=jnp.float32)
        return accumulated, (grad_blocks.reshape(SEQUENCE_LENGTH, E), grad_hid)

    accumulated, outputs = lax.scan(one_sequence, jnp.zeros((D, STATE), jnp.float32), (hidden_in, inner_acts, read_proj, step_size, log_decay, grad_fwd, grad_rev))
    return outputs[0], outputs[1], accumulated / (BATCH_SEQUENCES * SEQUENCE_LENGTH)
```

```python
import jax
import jax.numpy as jnp
from jax import lax
from jax.experimental import pallas as pl
from jax.experimental.pallas import tpu as pltpu
from jax.sharding import PartitionSpec as P

MESH = pl.DeviceIdType.MESH
F32 = jnp.float32
BF16 = jnp.bfloat16
HIGH = lax.Precision.HIGHEST
GROUP = ((2, 0), (1, 0), (3, 1), (1, 1), (3, 0), (2, 1), (0, 1))
ACROSS = ((2, 0), (0, 0), (1, 1), (3, 0), (1, 0), (3, 1), (2, 1), (0, 1))
ZPEERS = ((0, 1), (1, 0), (1, 1))
POSITIONS = 16384
(S_WA, S_WB, S_WC, S_WD, S_SMALL, S_FWD, S_REV, S_WRITE, S_INNER, S_TOTAL, S_GW, S_GI, S_R1, S_R2, S_R3, S_R4) = range(16)


def remote(src, dst, send_sem, recv_sem, device):
    copy = pltpu.make_async_remote_copy(
        src_ref=src, dst_ref=dst, send_sem=send_sem, recv_sem=recv_sem, device_id=device, device_id_type=MESH
    )
    copy.start()


def drain(ref, sem):
    pltpu.make_async_copy(ref, ref, sem).wait()


def dot(a, b, dims=((1,), (0,)), precision=None):
    return lax.dot_general(a, b, (dims, ((), ())), precision=precision, preferred_element_type=F32)


def body(
    scale_ref, weight_hbm, hidden_hbm, inner_hbm, read_hbm, step_hbm, decay_hbm, fwd_hbm, rev_hbm,
    gi_out, gh_out, gw_out,
    wraw, wnat, hid, fr, rr, br, ir, rd, st, dc, wr,
    row_c, row_e, col, fac, pf, qf, carry, run,
    r0, l0, rb, lb, tsend, trecv, es, gi, gws, gwr,
    gf, gb, rb1, hb, rb2, acc2, h3, rb3, acc3, h4, rb4, gh,
    ss, rs, rin, rr1, ls,
):
    dp, ctx = lax.axis_index("dp"), lax.axis_index("ctx")
    y, zl = dp // 2, dp % 2
    zh, x, k = ctx // 8, (ctx // 2) % 4, ctx % 2
    j = ctx % 8
    other = 1 - zh

    def at(dx, dk):
        return ((x + dx) % 4) * 2 + (k + dk) % 2

    def group(slot):
        return {"dp": dp, "ctx": zh * 8 + slot}

    def across(slot):
        return {"dp": dp, "ctx": other * 8 + slot}

    def xpeer(dx):
        return {"dp": dp, "ctx": zh * 8 + ((x + dx) % 4) * 2 + k}

    def ypeer(dy):
        return {"dp": ((y + dy) % 4) * 2 + zl, "ctx": ctx}

    def zpeer(dl, dh):
        return {"dp": y * 2 + (zl + dl) % 2, "ctx": ((zh + dh) % 2) * 8 + j}

    sibling = {"dp": dp, "ctx": zh * 8 + x * 2 + (1 - k)}

    wcopy = pltpu.make_async_copy(weight_hbm, wraw, ls.at[0])
    wcopy.start()
    hcopy = pltpu.make_async_copy(hidden_hbm, hid, ls.at[1])
    hcopy.start()

    barrier = pltpu.get_barrier_semaphore()
    peers = [group(at(*o)) for o in GROUP] + [across(at(*o)) for o in ACROSS]
    peers += [ypeer(d) for d in (1, 2, 3)] + [zpeer(1, 0), zpeer(1, 1)]
    for peer in peers:
        pl.semaphore_signal(barrier, inc=1, device_id=peer, device_id_type=MESH)
    pl.semaphore_wait(barrier, len(peers))

    own = dp * 8 + zh * 4 + x
    wcopy.wait()
    wnat[own, k] = (wraw[...].astype(F32) * scale_ref[0]).astype(BF16)

    for o in GROUP:
        t = at(*o)
        remote(step_hbm.at[pl.ds(pl.multiple_of(t * 8, 8), 8), :], st.at[j], ss.at[S_SMALL], rs.at[S_SMALL], group(t))
        remote(decay_hbm.at[pl.ds(pl.multiple_of(t * 8, 8), 8), :], dc.at[j], ss.at[S_SMALL + 16], rs.at[S_SMALL + 16], group(t))
    for dx in (1, 2, 3):
        remote(wnat.at[own, k], wnat.at[own, k], ss.at[S_WA], rs.at[S_WA], xpeer(dx))
    for o in GROUP:
        t = at(*o)
        remote(read_hbm, rd.at[j], ss.at[S_SMALL + 17], rs.at[S_SMALL + 17], group(t))
    own_rows = pl.ds(pl.multiple_of(j * 8, 8), 8)
    own_cols = pl.ds(pl.multiple_of(j * 512, 512), 512)
    pltpu.make_async_copy(step_hbm.at[own_rows, :], st.at[j], rs.at[S_SMALL]).start()
    pltpu.make_async_copy(decay_hbm.at[own_rows, :], dc.at[j], rs.at[S_SMALL + 16]).start()
    pltpu.make_async_copy(read_hbm, rd.at[j], rs.at[S_SMALL + 17]).start()
    for o in GROUP:
        t = at(*o)
        cols = pl.ds(pl.multiple_of(t * 512, 512), 512)
        remote(fwd_hbm.at[:, cols], fr.at[j], ss.at[S_FWD], rs.at[S_FWD], group(t))
    pltpu.make_async_copy(fwd_hbm.at[:, own_cols], fr.at[j], rs.at[S_FWD]).start()
    for o in ACROSS:
        t = at(*o)
        cols = pl.ds(pl.multiple_of(t * 512, 512), 512)
        remote(rev_hbm.at[:, cols], rr.at[7 - j], ss.at[S_REV], rs.at[S_REV], across(t))
    pltpu.make_async_copy(inner_hbm.at[:, own_cols], ir.at[j], rin.at[j]).start()

    drain(wnat.at[pl.ds(0, 3), 0], rs.at[S_WA])
    four = pl.ds(dp * 8 + zh * 4, 4)
    for dl, dh in ZPEERS:
        remote(wnat.at[four, k], wnat.at[four, k], ss.at[S_WB], rs.at[S_WB], zpeer(dl, dh))

    drain(st, rs.at[S_SMALL])
    drain(dc, rs.at[S_SMALL + 16])
    rows = lax.broadcasted_iota(jnp.int32, (128, 128), 0)
    lanes = lax.broadcasted_iota(jnp.int32, (128, 128), 1)
    upper = lanes >= rows
    lower = lanes <= rows
    first_half = lanes < 64
    decay = dc[...].reshape(64, 128)
    cum = dot(decay, upper.astype(F32), precision=HIGH)
    excl = cum - decay
    log_step = jnp.log(st[...].reshape(64, 128))
    end = jnp.sum(decay, axis=1, keepdims=True)
    end = jnp.broadcast_to(cum[:, 127:128], (64, 128))
    c1 = cum - log_step
    c2 = excl + log_step
    kinds = (c1, c2, jnp.exp(end - c1), jnp.exp(c2), jnp.exp(cum), jnp.exp(end - excl))
    row_c[...] = cum.reshape(8, 8, 128)
    row_e[...] = excl.reshape(8, 8, 128)
    block_decay = jnp.exp(end)
    head_of = lax.broadcasted_iota(jnp.int32, (8, 512), 1) // 64
    pick = head_of == lax.broadcasted_iota(jnp.int32, (8, 512), 0)
    pad = jnp.zeros((80, 128), F32)
    for b in range(8):
        part = [kind[8 * b : 8 * b + 8] for kind in kinds]
        col[b] = jnp.transpose(jnp.concatenate(part + [pad], axis=0))
        wide = jnp.where(pick, jnp.broadcast_to(block_decay[8 * b : 8 * b + 8, 0:1], (8, 512)), 0.0)
        fac[b] = jnp.broadcast_to(jnp.sum(wide, axis=0, keepdims=True), (8, 512))

    drain(wnat.at[pl.ds(0, 12), 0], rs.at[S_WB])
    sixteen = pl.ds(y * 16, 16)
    for dy in (2, 1, 3):
        remote(wnat.at[sixteen, k], wnat.at[sixteen, k], ss.at[S_WC], rs.at[S_WC], ypeer(dy))

    def column(b, index):
        return jnp.broadcast_to(col[b, :, index : index + 1], (128, 128))

    drain(rd, rs.at[S_SMALL + 17])
    drain(fr, rs.at[S_FWD])
    carry[...] = jnp.zeros_like(carry)
    run[...] = jnp.ones_like(run)

    def right_step(i, _):
        b = 7 - i
        pf[b] = run[...]
        run[...] = run[...] * fac[b]
        for p in range(4):
            sl = slice(128 * p, 128 * p + 128)
            w = jnp.where(first_half, column(b, 32 + 2 * p), column(b, 33 + 2 * p))
            scaled = (fr[b, :, sl].astype(F32) * w).astype(BF16)
            part = dot(rd[b], scaled, ((0,), (0,)))
            old = carry[:, sl]
            r0[b, :, sl] = old
            carry[:, sl] = part + fac[b, 0:1, sl] * old
        return 0

    lax.fori_loop(0, 8, right_step, 0)

    drain(wnat.at[pl.ds(0, 48), 0], rs.at[S_WC])
    remote(wnat.at[:, k], wnat.at[:, k], ss.at[S_WD], rs.at[S_WD], sibling)
    hcopy.wait()
    drain(wnat.at[:, 0], rs.at[S_WD])
    write = jnp.zeros((128, 128), F32)
    for c in range(8):
        write += dot(hid[:, 512 * c : 512 * c + 512], wnat[8 * c : 8 * c + 8].reshape(512, 128))
    wr[j] = write.astype(BF16)

    @pl.when(zh == 1)
    def _():
        tsend[...] = carry[...].astype(BF16)

    for o in GROUP:
        t = at(*o)
        remote(wr.at[j], wr.at[j], ss.at[S_WRITE], rs.at[S_WRITE], group(t))
    for o in GROUP:
        t = at(*o)
        cols = pl.ds(pl.multiple_of(t * 512, 512), 512)
        remote(inner_hbm.at[:, cols], ir.at[j], ss.at[S_INNER], rin.at[j], group(t))

    drain(rr, rs.at[S_REV])
    carry[...] = jnp.zeros_like(carry)
    run[...] = jnp.ones_like(run)
    flip = (rows + lanes == 127).astype(F32).astype(BF16)

    def left_step(b, _):
        qf[b] = run[...]
        run[...] = run[...] * fac[b]
        for p in range(4):
            sl = slice(128 * p, 128 * p + 128)
            back = dot(flip, rr[b, :, sl])
            br[b, :, sl] = back.astype(BF16)
            w = jnp.where(first_half, column(b, 40 + 2 * p), column(b, 41 + 2 * p))
            part = dot(rd[b], (back * w).astype(BF16), ((0,), (0,)))
            old = carry[:, sl]
            l0[b, :, sl] = old
            carry[:, sl] = part + fac[b, 0:1, sl] * old
        return 0

    lax.fori_loop(0, 8, left_step, 0)

    @pl.when(zh == 0)
    def _():
        tsend[...] = carry[...].astype(BF16)

    remote(tsend, trecv, ss.at[S_TOTAL], rs.at[S_TOTAL], across(j))

    def decay_step(b, _):
        for h in range(8):
            arg = jnp.where(upper, row_c[b, h : h + 1, :] - column(b, h), column(b, 8 + h) - row_e[b, h : h + 1, :])
            es[b, h] = jnp.exp(arg)
        return 0

    lax.fori_loop(0, 8, decay_step, 0)

    drain(trecv, rs.at[S_TOTAL])
    low = (1 - zh).astype(F32)
    high = zh.astype(F32)

    def edge_step(b, _):
        far = trecv[...].astype(F32)
        rb[b] = (r0[b] + (pf[b, 0:1, :] * low) * far).astype(BF16)
        lb[b] = (l0[b] + (qf[b, 0:1, :] * high) * far).astype(BF16)
        return 0

    lax.fori_loop(0, 8, edge_step, 0)

    drain(wr.at[pl.ds(0, 7)], rs.at[S_WRITE])

    def stacked(b, sl):
        return jnp.concatenate([fr[b, :, sl], br[b, :, sl], rb[b, :, sl], lb[b, :, sl]], axis=0)

    def inner_grad_step(b, _):
        kern = dot(wr[b], rd[b], ((1,), (1,)))
        wf = wr[b].astype(F32)
        for p in range(4):
            sl = slice(128 * p, 128 * p + 128)
            mixes = []
            for h in (2 * p, 2 * p + 1):
                e = es[b, h]
                mixes.append(
                    jnp.concatenate(
                        [
                            (jnp.where(upper, e, 0.0) * kern).astype(BF16),
                            (jnp.where(lower, e, 0.0) * kern).astype(BF16),
                            (column(b, 16 + h) * wf).astype(BF16),
                            (column(b, 24 + h) * wf).astype(BF16),
                        ],
                        axis=1,
                    )
                )
            out = dot(jnp.concatenate(mixes, axis=0), stacked(b, sl))
            gi[b, :, sl] = jnp.where(first_half, out[:128], out[128:]).astype(BF16)
        return 0

    lax.fori_loop(0, 8, inner_grad_step, 0)

    half = first_half.astype(F32)
    mask_a = half.astype(BF16)
    mask_b = (1.0 - half).astype(BF16)

    def write_grad_step(i, _):
        b = at(i // 2, i % 2)
        drain(ir.at[0], rin.at[b])
        mixed = jnp.zeros((128, 128), F32)
        edge = jnp.zeros((128, 128), F32)
        for p in range(4):
            sl = slice(128 * p, 128 * p + 128)
            act = ir[b, :, sl]
            dots = dot(jnp.concatenate([act * mask_a, act * mask_b], axis=0), stacked(b, sl), ((1,), (1,)))
            for a in range(2):
                h = 2 * p + a
                d = dots[128 * a : 128 * a + 128]
                e = es[b, h]
                mixed += jnp.where(upper, e, 0.0) * d[:, :128] + jnp.where(lower, e, 0.0) * d[:, 128:256]
                edge += column(b, 16 + h) * d[:, 256:384] + column(b, 24 + h) * d[:, 384:]
        part = (dot(mixed.astype(BF16), rd[b]) + edge).astype(BF16)
        gws[b] = part

        @pl.when(i == 0)
        def _():
            gwr[b] = part

        @pl.when(i > 0)
        def _():
            remote(gws.at[b], gwr.at[j], ss.at[S_GW], rs.at[S_GW], group(b))

        return 0

    lax.fori_loop(0, 8, write_grad_step, 0)

    for o in GROUP:
        t = at(*o)
        remote(gi.at[t], gi_out.at[:, own_cols], ss.at[S_GI], rs.at[S_GI], group(t))
    pltpu.make_async_copy(gi.at[j], gi_out.at[:, own_cols], rs.at[S_GI]).start()

    drain(gwr.at[pl.ds(0, 7)], rs.at[S_GW])
    total = gwr[0].astype(F32)
    for b in range(1, 8):
        total += gwr[b].astype(F32)
    wb = total.astype(BF16)

    for c in range(8):
        piece = dot(hid[:, 512 * c : 512 * c + 512], wb, ((0,), (0,)))
        gf[8 * c : 8 * c + 8] = piece.reshape(8, 2, 32, 128)
    order = (2, 1, 3, 0)
    for dy in order:
        part = pl.ds(((y + dy) % 4) * 16, 16)
        gb[part] = gf[part, 1 - k].astype(BF16)
    for n, dy in enumerate(order):
        part = pl.ds(((y + dy) % 4) * 16, 16)
        remote(gb.at[part], rb1.at[part], ss.at[S_R1], rr1.at[n], sibling)
    for n, dy in enumerate(order):
        part = pl.ds(((y + dy) % 4) * 16, 16)
        drain(rb1.at[pl.ds(0, 16)], rr1.at[n])
        both = gf[part, k] + rb1[part].astype(F32)
        if dy:
            hb[dy - 1] = both.astype(BF16)
            remote(hb.at[dy - 1], rb2.at[dy - 1], ss.at[S_R2], rs.at[S_R2], ypeer(dy))
        else:
            acc2[...] = both

    for c in range(8):
        rows_c = wnat[8 * c : 8 * c + 8].reshape(512, 128)
        gh[:, 512 * c : 512 * c + 512] = dot(wb, rows_c, ((1,), (1,))).astype(BF16)
    ghcopy = pltpu.make_async_copy(gh, gh_out, ls.at[2])
    ghcopy.start()

    drain(rb2, rs.at[S_R2])
    acc2[...] = acc2[...] + (rb2[0].astype(F32) + rb2[1].astype(F32) + rb2[2].astype(F32))
    for n, (dl, dh) in enumerate(ZPEERS):
        part = pl.ds((((zl + dl) % 2) * 2 + (zh + dh) % 2) * 4, 4)
        h3[n] = acc2[part].astype(BF16)
        remote(h3.at[n], rb3.at[n], ss.at[S_R3], rs.at[S_R3], zpeer(dl, dh))
    drain(rb3, rs.at[S_R3])
    acc3[...] = acc2[pl.ds((zl * 2 + zh) * 4, 4)] + (rb3[0].astype(F32) + rb3[1].astype(F32) + rb3[2].astype(F32))
    for dx in (1, 2, 3):
        h4[dx - 1] = acc3[(x + dx) % 4].astype(BF16)
        remote(h4.at[dx - 1], rb4.at[dx - 1], ss.at[S_R4], rs.at[S_R4], xpeer(dx))
    drain(rb4, rs.at[S_R4])
    gw_out[...] = (acc3[x] + (rb4[0].astype(F32) + rb4[1].astype(F32) + rb4[2].astype(F32))) * (1.0 / POSITIONS)

    drain(wnat.at[pl.ds(0, 3), 0], ss.at[S_WA])
    drain(wnat.at[pl.ds(0, 12), 0], ss.at[S_WB])
    drain(wnat.at[pl.ds(0, 48), 0], ss.at[S_WC])
    drain(wnat.at[:, 0], ss.at[S_WD])
    drain(st.at[pl.ds(0, 7)], ss.at[S_SMALL])
    drain(dc.at[pl.ds(0, 7)], ss.at[S_SMALL + 16])
    drain(rd.at[pl.ds(0, 7)], ss.at[S_SMALL + 17])
    drain(fr.at[pl.ds(0, 7)], ss.at[S_FWD])
    drain(rr, ss.at[S_REV])
    drain(wr.at[pl.ds(0, 7)], ss.at[S_WRITE])
    drain(ir.at[pl.ds(0, 7)], ss.at[S_INNER])
    drain(tsend, ss.at[S_TOTAL])
    drain(gws.at[pl.ds(0, 7)], ss.at[S_GW])
    drain(gi.at[pl.ds(0, 7)], ss.at[S_GI])
    drain(gb, ss.at[S_R1])
    drain(hb, ss.at[S_R2])
    drain(h3, ss.at[S_R3])
    drain(h4, ss.at[S_R4])
    ghcopy.wait()
    drain(gi, rs.at[S_GI])


def shards(hidden, weight, scale, inner, read, step, decay, fwd, rev):
    hbm = pl.BlockSpec(memory_space=pl.ANY)
    vm = pltpu.VMEM
    gi, gh, gw = pl.pallas_call(
        body,
        out_shape=(
            jax.ShapeDtypeStruct((128, 4096), BF16),
            jax.ShapeDtypeStruct((128, 4096), BF16),
            jax.ShapeDtypeStruct((32, 128), F32),
        ),
        in_specs=[pl.BlockSpec(memory_space=pltpu.SMEM)] + [hbm] * 8,
        out_specs=(hbm, hbm, pl.BlockSpec(memory_space=pltpu.VMEM)),
        scratch_shapes=[
            vm((32, 128), BF16),
            vm((64, 2, 32, 128), BF16),
            vm((128, 4096), BF16),
            vm((8, 128, 512), BF16),
            vm((8, 128, 512), BF16),
            vm((8, 128, 512), BF16),
            vm((8, 128, 512), BF16),
            vm((8, 128, 128), BF16),
            vm((8, 8, 128), F32),
            vm((8, 8, 128), F32),
            vm((8, 128, 128), BF16),
            vm((8, 8, 128), F32),
            vm((8, 8, 128), F32),
            vm((8, 128, 128), F32),
            vm((8, 8, 512), F32),
            vm((8, 8, 512), F32),
            vm((8, 8, 512), F32),
            vm((128, 512), F32),
            vm((8, 512), F32),
            vm((8, 128, 512), F32),
            vm((8, 128, 512), F32),
            vm((8, 128, 512), BF16),
            vm((8, 128, 512), BF16),
            vm((128, 512), BF16),
            vm((128, 512), BF16),
            vm((8, 8, 128, 128), F32),
            vm((8, 128, 512), BF16),
            vm((8, 128, 128), BF16),
            vm((8, 128, 128), BF16),
            vm((64, 2, 32, 128), F32),
            vm((64, 32, 128), BF16),
            vm((64, 32, 128), BF16),
            vm((3, 16, 32, 128), BF16),
            vm((3, 16, 32, 128), BF16),
            vm((16, 32, 128), F32),
            vm((3, 4, 32, 128), BF16),
            vm((3, 4, 32, 128), BF16),
            vm((4, 32, 128), F32),
            vm((3, 32, 128), BF16),
            vm((3, 32, 128), BF16),
            vm((128, 4096), BF16),
            pltpu.SemaphoreType.DMA((34,)),
            pltpu.SemaphoreType.DMA((34,)),
            pltpu.SemaphoreType.DMA((8,)),
            pltpu.SemaphoreType.DMA((4,)),
            pltpu.SemaphoreType.DMA((3,)),
        ],
        compiler_params=pltpu.CompilerParams(
            collective_id=0, has_side_effects=True, vmem_limit_bytes=60 * 1024 * 1024
        ),
        name="layer_backward",
    )(scale, weight, hidden[0], inner[0], read[0], step[0], decay[0], fwd[0], rev[0])
    return gi[None], gh[None], gw


def solution(mesh):
    in_specs = (
        P("dp", "ctx", None),
        P(("dp", "ctx"), None),
        P(("dp", "ctx")),
        P("dp", "ctx", None),
        P("dp", "ctx", None),
        P("dp", None, "ctx"),
        P("dp", None, "ctx"),
        P("dp", "ctx", None),
        P("dp", "ctx", None),
    )
    out_specs = (P("dp", "ctx", None), P("dp", "ctx", None), P(("dp", "ctx"), None))
    return jax.shard_map(shards, mesh=mesh, in_specs=in_specs, out_specs=out_specs, check_vma=False)
```

```python
import jax
import jax.numpy as jnp
from jax import lax
from jax.experimental import pallas as pl
from jax.experimental.pallas import tpu as pltpu
from jax.sharding import PartitionSpec as P

MESH = pl.DeviceIdType.MESH
F32 = jnp.float32
BF16 = jnp.bfloat16
HIGH = lax.Precision.HIGHEST
GROUP = ((0, 1), (3, 0), (1, 0), (3, 1), (1, 1), (2, 0), (2, 1))
ACROSS = ((2, 0), (0, 0), (1, 1), (3, 0), (1, 0), (3, 1), (2, 1), (0, 1))
ISSUE = tuple(
    (name[0], int(name[1])) for name in "f0 f1 f2 r0 f3 r1 f4 r2 f5 r3 f6 r4 r5 r6 r7".split()
)
ZPEERS = ((0, 1), (1, 0), (1, 1))
POSITIONS = 16384
(
    S_WA, S_WB, S_WC, S_WD, S_STEP, S_DECAY, S_READ, S_READ2, S_FWD, S_REV, S_WRITE, S_WRITE2, S_INNER, S_TOTAL,
    S_GW, S_GI, S_HT, S_WBX, S_A1, S_B1, S_A2, S_B2, S_X,
) = range(23)


def remote(src, dst, send_sem, recv_sem, device):
    copy = pltpu.make_async_remote_copy(
        src_ref=src, dst_ref=dst, send_sem=send_sem, recv_sem=recv_sem, device_id=device, device_id_type=MESH
    )
    copy.start()


def drain(ref, sem):
    pltpu.make_async_copy(ref, ref, sem).wait()


def dot(a, b, dims=((1,), (0,)), precision=None):
    return lax.dot_general(a, b, (dims, ((), ())), precision=precision, preferred_element_type=F32)


def body(
    scale_ref, weight_hbm, hidden_hbm, inner_hbm, read_hbm, step_hbm, decay_hbm, fwd_hbm, rev_hbm,
    gi_out, gh_out, gw_out,
    wraw, wnat, hid, fr, rr, br, ir, rd, st, dc, wr,
    row_c, row_e, col, fac, pf, qf, carry, run,
    r0, l0, rb, lb, tsend, trecv, es, gi, gws, gwr,
    ht, hsib, wbs, wbr, gf, gb, ra1, rb1, acca, accb, ha, ra2, hb, rb2, accx, hx, rx, gh,
    ss, rs, rin, ls,
):
    dp, ctx = lax.axis_index("dp"), lax.axis_index("ctx")
    y, zl = dp // 2, dp % 2
    zh, x, k = ctx // 8, (ctx // 2) % 4, ctx % 2
    j = ctx % 8
    other = 1 - zh

    def at(dx, dk):
        return ((x + dx) % 4) * 2 + (k + dk) % 2

    def group(slot):
        return {"dp": dp, "ctx": zh * 8 + slot}

    def across(slot):
        return {"dp": dp, "ctx": other * 8 + slot}

    def xpeer(dx):
        return {"dp": dp, "ctx": zh * 8 + ((x + dx) % 4) * 2 + k}

    def ypeer(dy):
        return {"dp": ((y + dy) % 4) * 2 + zl, "ctx": ctx}

    def zpeer(dl, dh):
        return {"dp": y * 2 + (zl + dl) % 2, "ctx": ((zh + dh) % 2) * 8 + j}

    sibling = {"dp": dp, "ctx": zh * 8 + x * 2 + (1 - k)}

    wcopy = pltpu.make_async_copy(weight_hbm, wraw, ls.at[0])
    wcopy.start()
    hcopy = pltpu.make_async_copy(hidden_hbm, hid, ls.at[1])
    hcopy.start()

    barrier = pltpu.get_barrier_semaphore()
    peers = [group(at(*o)) for o in GROUP] + [across(at(*o)) for o in ACROSS]
    peers += [ypeer(d) for d in (1, 2, 3)] + [zpeer(1, 0), zpeer(1, 1)]
    for peer in peers:
        pl.semaphore_signal(barrier, inc=1, device_id=peer, device_id_type=MESH)
    pl.semaphore_wait(barrier, len(peers))

    own = dp * 8 + zh * 4 + x
    wcopy.wait()
    wnat[own, k] = (wraw[...].astype(F32) * scale_ref[0]).astype(BF16)

    for o in GROUP:
        t = at(*o)
        remote(step_hbm.at[pl.ds(pl.multiple_of(t * 8, 8), 8), :], st.at[j], ss.at[S_STEP], rs.at[S_STEP], group(t))
        remote(decay_hbm.at[pl.ds(pl.multiple_of(t * 8, 8), 8), :], dc.at[j], ss.at[S_DECAY], rs.at[S_DECAY], group(t))
    for dx in (1, 2, 3):
        remote(wnat.at[own, k], wnat.at[own, k], ss.at[S_WA], rs.at[S_WA], xpeer(dx))
    for dx in (1, 2, 3):
        remote(read_hbm, rd.at[x, k], ss.at[S_READ], rs.at[S_READ], xpeer(dx))
    own_rows = pl.ds(pl.multiple_of(j * 8, 8), 8)
    own_cols = pl.ds(pl.multiple_of(j * 512, 512), 512)
    pltpu.make_async_copy(step_hbm.at[own_rows, :], st.at[j], rs.at[S_STEP]).start()
    pltpu.make_async_copy(decay_hbm.at[own_rows, :], dc.at[j], rs.at[S_DECAY]).start()
    pltpu.make_async_copy(read_hbm, rd.at[x, k], rs.at[S_READ]).start()
    pltpu.make_async_copy(fwd_hbm.at[:, own_cols], fr.at[j], rs.at[S_FWD]).start()
    for strand, n in ISSUE:
        t = at(*(GROUP[n] if strand == "f" else ACROSS[n]))
        cols = pl.ds(pl.multiple_of(t * 512, 512), 512)
        if strand == "f":
            remote(fwd_hbm.at[:, cols], fr.at[j], ss.at[S_FWD], rs.at[S_FWD], group(t))
        else:
            remote(rev_hbm.at[:, cols], rr.at[7 - j], ss.at[S_REV], rs.at[S_REV], across(t))
    pltpu.make_async_copy(inner_hbm.at[:, own_cols], ir.at[j], rin.at[j]).start()

    drain(wnat.at[pl.ds(0, 3), 0], rs.at[S_WA])
    four = pl.ds(dp * 8 + zh * 4, 4)
    for dl, dh in ZPEERS:
        remote(wnat.at[four, k], wnat.at[four, k], ss.at[S_WB], rs.at[S_WB], zpeer(dl, dh))

    drain(st, rs.at[S_STEP])
    drain(dc, rs.at[S_DECAY])
    rows = lax.broadcasted_iota(jnp.int32, (128, 128), 0)
    lanes = lax.broadcasted_iota(jnp.int32, (128, 128), 1)
    upper = lanes >= rows
    lower = lanes <= rows
    first_half = lanes < 64
    decay = dc[...].reshape(64, 128)
    cum = dot(decay, upper.astype(F32), precision=HIGH)
    excl = cum - decay
    log_step = jnp.log(st[...].reshape(64, 128))
    end = jnp.broadcast_to(cum[:, 127:128], (64, 128))
    c1 = cum - log_step
    c2 = excl + log_step
    kinds = (c1, c2, jnp.exp(end - c1), jnp.exp(c2), jnp.exp(cum), jnp.exp(end - excl))
    row_c[...] = cum.reshape(8, 8, 128)
    row_e[...] = excl.reshape(8, 8, 128)
    block_decay = jnp.exp(end)
    head_of = lax.broadcasted_iota(jnp.int32, (8, 512), 1) // 64
    pick = head_of == lax.broadcasted_iota(jnp.int32, (8, 512), 0)
    pad = jnp.zeros((80, 128), F32)
    for b in range(8):
        part = [kind[8 * b : 8 * b + 8] for kind in kinds]
        col[b] = jnp.transpose(jnp.concatenate(part + [pad], axis=0))
        wide = jnp.where(pick, jnp.broadcast_to(block_decay[8 * b : 8 * b + 8, 0:1], (8, 512)), 0.0)
        fac[b] = jnp.broadcast_to(jnp.sum(wide, axis=0, keepdims=True), (8, 512))

    drain(wnat.at[pl.ds(0, 12), 0], rs.at[S_WB])
    sixteen = pl.ds(y * 16, 16)
    for dy in (2, 1, 3):
        remote(wnat.at[sixteen, k], wnat.at[sixteen, k], ss.at[S_WC], rs.at[S_WC], ypeer(dy))

    def column(b, index):
        return jnp.broadcast_to(col[b, :, index : index + 1], (128, 128))

    def decay_step(b, _):
        for h in range(8):
            arg = jnp.where(upper, row_c[b, h : h + 1, :] - column(b, h), column(b, 8 + h) - row_e[b, h : h + 1, :])
            es[b, h] = jnp.exp(arg)
        return 0

    lax.fori_loop(0, 8, decay_step, 0)

    drain(rd.at[:, 0], rs.at[S_READ])
    remote(rd.at[:, k], rd.at[:, k], ss.at[S_READ2], rs.at[S_READ2], sibling)

    hcopy.wait()
    for c in range(8):
        turned = jnp.transpose(hid[:, 512 * c : 512 * c + 512])
        ht[8 * c : 8 * c + 8] = turned.reshape(8, 2, 32, 128)

    drain(wnat.at[pl.ds(0, 48), 0], rs.at[S_WC])
    remote(wnat.at[:, k], wnat.at[:, k], ss.at[S_WD], rs.at[S_WD], sibling)
    remote(ht.at[:, 1 - k], hsib, ss.at[S_HT], rs.at[S_HT], sibling)

    drain(rd.at[:, 0], rs.at[S_READ2])
    drain(fr, rs.at[S_FWD])
    carry[...] = jnp.zeros_like(carry)
    run[...] = jnp.ones_like(run)

    def right_step(i, _):
        b = 7 - i
        pf[b] = run[...]
        run[...] = run[...] * fac[b]
        for p in range(4):
            sl = slice(128 * p, 128 * p + 128)
            w = jnp.where(first_half, column(b, 32 + 2 * p), column(b, 33 + 2 * p))
            scaled = (fr[b, :, sl].astype(F32) * w).astype(BF16)
            part = dot(rd[b // 2, b % 2], scaled, ((0,), (0,)))
            old = carry[:, sl]
            r0[b, :, sl] = old
            carry[:, sl] = part + fac[b, 0:1, sl] * old
        return 0

    lax.fori_loop(0, 8, right_step, 0)

    drain(wnat.at[:, 0], rs.at[S_WD])
    write = jnp.zeros((128, 128), F32)
    for c in range(8):
        write += dot(hid[:, 512 * c : 512 * c + 512], wnat[8 * c : 8 * c + 8].reshape(512, 128))
    wr[x, k] = write.astype(BF16)

    @pl.when(zh == 1)
    def _():
        tsend[...] = carry[...].astype(BF16)

    for dx in (1, 2, 3):
        remote(wr.at[x, k], wr.at[x, k], ss.at[S_WRITE], rs.at[S_WRITE], xpeer(dx))
    for o in GROUP:
        t = at(*o)
        cols = pl.ds(pl.multiple_of(t * 512, 512), 512)
        remote(inner_hbm.at[:, cols], ir.at[j], ss.at[S_INNER], rin.at[j], group(t))

    drain(rr, rs.at[S_REV])
    drain(wr.at[pl.ds(0, 3), 0], rs.at[S_WRITE])
    remote(wr.at[:, k], wr.at[:, k], ss.at[S_WRITE2], rs.at[S_WRITE2], sibling)
    carry[...] = jnp.zeros_like(carry)
    run[...] = jnp.ones_like(run)
    flip = (rows + lanes == 127).astype(F32).astype(BF16)

    def left_step(b, _):
        qf[b] = run[...]
        run[...] = run[...] * fac[b]
        for p in range(4):
            sl = slice(128 * p, 128 * p + 128)
            back = dot(flip, rr[b, :, sl])
            br[b, :, sl] = back.astype(BF16)
            w = jnp.where(first_half, column(b, 40 + 2 * p), column(b, 41 + 2 * p))
            part = dot(rd[b // 2, b % 2], (back * w).astype(BF16), ((0,), (0,)))
            old = carry[:, sl]
            l0[b, :, sl] = old
            carry[:, sl] = part + fac[b, 0:1, sl] * old
        return 0

    lax.fori_loop(0, 8, left_step, 0)

    @pl.when(zh == 0)
    def _():
        tsend[...] = carry[...].astype(BF16)

    remote(tsend, trecv, ss.at[S_TOTAL], rs.at[S_TOTAL], across(j))

    drain(trecv, rs.at[S_TOTAL])
    low = (1 - zh).astype(F32)
    high = zh.astype(F32)

    def edge_step(b, _):
        far = trecv[...].astype(F32)
        rb[b] = (r0[b] + (pf[b, 0:1, :] * low) * far).astype(BF16)
        lb[b] = (l0[b] + (qf[b, 0:1, :] * high) * far).astype(BF16)
        return 0

    lax.fori_loop(0, 8, edge_step, 0)

    drain(wr.at[:, 0], rs.at[S_WRITE2])

    def stacked(b, sl):
        return jnp.concatenate([fr[b, :, sl], br[b, :, sl], rb[b, :, sl], lb[b, :, sl]], axis=0)

    def inner_grad_step(b, _):
        kern = dot(wr[b // 2, b % 2], rd[b // 2, b % 2], ((1,), (1,)))
        wf = wr[b // 2, b % 2].astype(F32)
        for p in range(4):
            sl = slice(128 * p, 128 * p + 128)
            mixes = []
            for h in (2 * p, 2 * p + 1):
                e = es[b, h]
                mixes.append(
                    jnp.concatenate(
                        [
                            (jnp.where(upper, e, 0.0) * kern).astype(BF16),
                            (jnp.where(lower, e, 0.0) * kern).astype(BF16),
                            (column(b, 16 + h) * wf).astype(BF16),
                            (column(b, 24 + h) * wf).astype(BF16),
                        ],
                        axis=1,
                    )
                )
            out = dot(jnp.concatenate(mixes, axis=0), stacked(b, sl))
            gi[b, :, sl] = jnp.where(first_half, out[:128], out[128:]).astype(BF16)
        return 0

    lax.fori_loop(0, 8, inner_grad_step, 0)

    half = first_half.astype(F32)
    mask_a = half.astype(BF16)
    mask_b = (1.0 - half).astype(BF16)

    def write_grad_step(i, _):
        q = i // 2
        b = at((q * (q + 1) // 2) % 4, i % 2)
        drain(ir.at[0], rin.at[b])
        mixed = jnp.zeros((128, 128), F32)
        edge = jnp.zeros((128, 128), F32)
        for p in range(4):
            sl = slice(128 * p, 128 * p + 128)
            act = ir[b, :, sl]
            dots = dot(jnp.concatenate([act * mask_a, act * mask_b], axis=0), stacked(b, sl), ((1,), (1,)))
            for a in range(2):
                h = 2 * p + a
                d = dots[128 * a : 128 * a + 128]
                e = es[b, h]
                mixed += jnp.where(upper, e, 0.0) * d[:, :128] + jnp.where(lower, e, 0.0) * d[:, 128:256]
                edge += column(b, 16 + h) * d[:, 256:384] + column(b, 24 + h) * d[:, 384:]
        part = (dot(mixed.astype(BF16), rd[b // 2, b % 2]) + edge).astype(BF16)
        gws[b] = part

        @pl.when(i == 0)
        def _():
            gwr[b] = part

        @pl.when(i > 0)
        def _():
            remote(gws.at[b], gwr.at[j], ss.at[S_GW], rs.at[S_GW], group(b))

        return 0

    lax.fori_loop(0, 8, write_grad_step, 0)

    for o in GROUP:
        t = at(*o)
        remote(gi.at[t], gi_out.at[:, own_cols], ss.at[S_GI], rs.at[S_GI], group(t))
    pltpu.make_async_copy(gi.at[j], gi_out.at[:, own_cols], rs.at[S_GI]).start()

    drain(gwr.at[pl.ds(0, 7)], rs.at[S_GW])
    total = gwr[0].astype(F32)
    for b in range(1, 8):
        total += gwr[b].astype(F32)
    wb = total.astype(BF16)

    wbs[...] = wb
    remote(wbs, wbr, ss.at[S_WBX], rs.at[S_WBX], sibling)

    drain(hsib, rs.at[S_HT])
    drain(wbr, rs.at[S_WBX])
    wbo = wbr[...]
    for dy in (2, 1, 3, 0):
        yt = (y + dy) % 4
        part = pl.ds(yt * 16, 16)
        piece = dot(ht[part, k].reshape(512, 128), wb) + dot(hsib[part].reshape(512, 128), wbo)
        piece = piece.reshape(4, 4, 32, 128)
        gf[yt] = piece
        gb[yt] = piece.astype(BF16)
        if dy:
            remote(gb.at[yt, :, :, pl.ds(0, 16)], ra1.at[dy - 1], ss.at[S_A1], rs.at[S_A1], ypeer(dy))
    zown = zl * 2 + zh
    zts = [((zl + dl) % 2) * 2 + (zh + dh) % 2 for dl, dh in ZPEERS]
    for n, (dl, dh) in enumerate(ZPEERS):
        remote(gb.at[:, zts[n], :, pl.ds(16, 16)], rb1.at[n], ss.at[S_B1], rs.at[S_B1], zpeer(dl, dh))

    for c in range(8):
        rows_c = wnat[8 * c : 8 * c + 8].reshape(512, 128)
        gh[:, 512 * c : 512 * c + 512] = dot(wb, rows_c, ((1,), (1,))).astype(BF16)
    ghcopy = pltpu.make_async_copy(gh, gh_out, ls.at[2])
    ghcopy.start()

    drain(ra1, rs.at[S_A1])
    acca[...] = gf[y, :, :, :16] + (ra1[0].astype(F32) + ra1[1].astype(F32) + ra1[2].astype(F32))
    for n, (dl, dh) in enumerate(ZPEERS):
        ha[n] = acca[zts[n]].astype(BF16)
        remote(ha.at[n], ra2.at[n], ss.at[S_A2], rs.at[S_A2], zpeer(dl, dh))
    drain(rb1, rs.at[S_B1])
    accb[...] = gf[:, zown, :, 16:] + (rb1[0].astype(F32) + rb1[1].astype(F32) + rb1[2].astype(F32))
    for dy in (2, 1, 3):
        hb[dy - 1] = accb[(y + dy) % 4].astype(BF16)
        remote(hb.at[dy - 1], rb2.at[dy - 1], ss.at[S_B2], rs.at[S_B2], ypeer(dy))
    drain(ra2, rs.at[S_A2])
    accx[:, :16] = acca[zown] + (ra2[0].astype(F32) + ra2[1].astype(F32) + ra2[2].astype(F32))
    drain(rb2, rs.at[S_B2])
    accx[:, 16:] = accb[y] + (rb2[0].astype(F32) + rb2[1].astype(F32) + rb2[2].astype(F32))
    for dx in (1, 2, 3):
        hx[dx - 1] = accx[(x + dx) % 4].astype(BF16)
        remote(hx.at[dx - 1], rx.at[dx - 1], ss.at[S_X], rs.at[S_X], xpeer(dx))
    drain(rx, rs.at[S_X])
    gw_out[...] = (accx[x] + (rx[0].astype(F32) + rx[1].astype(F32) + rx[2].astype(F32))) * (1.0 / POSITIONS)

    drain(wnat.at[pl.ds(0, 3), 0], ss.at[S_WA])
    drain(wnat.at[pl.ds(0, 12), 0], ss.at[S_WB])
    drain(wnat.at[pl.ds(0, 48), 0], ss.at[S_WC])
    drain(wnat.at[:, 0], ss.at[S_WD])
    drain(st.at[pl.ds(0, 7)], ss.at[S_STEP])
    drain(dc.at[pl.ds(0, 7)], ss.at[S_DECAY])
    drain(rd.at[pl.ds(0, 3), 0], ss.at[S_READ])
    drain(rd.at[:, 0], ss.at[S_READ2])
    drain(hsib, ss.at[S_HT])
    drain(wbs, ss.at[S_WBX])
    drain(fr.at[pl.ds(0, 7)], ss.at[S_FWD])
    drain(rr, ss.at[S_REV])
    drain(wr.at[pl.ds(0, 3), 0], ss.at[S_WRITE])
    drain(wr.at[:, 0], ss.at[S_WRITE2])
    drain(ir.at[pl.ds(0, 7)], ss.at[S_INNER])
    drain(tsend, ss.at[S_TOTAL])
    drain(gws.at[pl.ds(0, 7)], ss.at[S_GW])
    drain(gi.at[pl.ds(0, 7)], ss.at[S_GI])
    drain(ra1, ss.at[S_A1])
    drain(rb1, ss.at[S_B1])
    drain(ha, ss.at[S_A2])
    drain(hb, ss.at[S_B2])
    drain(hx, ss.at[S_X])
    ghcopy.wait()
    drain(gi, rs.at[S_GI])


def shards(hidden, weight, scale, inner, read, step, decay, fwd, rev):
    hbm = pl.BlockSpec(memory_space=pl.ANY)
    vm = pltpu.VMEM
    gi, gh, gw = pl.pallas_call(
        body,
        out_shape=(
            jax.ShapeDtypeStruct((128, 4096), BF16),
            jax.ShapeDtypeStruct((128, 4096), BF16),
            jax.ShapeDtypeStruct((32, 128), F32),
        ),
        in_specs=[pl.BlockSpec(memory_space=pltpu.SMEM)] + [hbm] * 8,
        out_specs=(hbm, hbm, pl.BlockSpec(memory_space=pltpu.VMEM)),
        scratch_shapes=[
            vm((32, 128), BF16),
            vm((64, 2, 32, 128), BF16),
            vm((128, 4096), BF16),
            vm((8, 128, 512), BF16),
            vm((8, 128, 512), BF16),
            vm((8, 128, 512), BF16),
            vm((8, 128, 512), BF16),
            vm((4, 2, 128, 128), BF16),
            vm((8, 8, 128), F32),
            vm((8, 8, 128), F32),
            vm((4, 2, 128, 128), BF16),
            vm((8, 8, 128), F32),
            vm((8, 8, 128), F32),
            vm((8, 128, 128), F32),
            vm((8, 8, 512), F32),
            vm((8, 8, 512), F32),
            vm((8, 8, 512), F32),
            vm((128, 512), F32),
            vm((8, 512), F32),
            vm((8, 128, 512), F32),
            vm((8, 128, 512), F32),
            vm((8, 128, 512), BF16),
            vm((8, 128, 512), BF16),
            vm((128, 512), BF16),
            vm((128, 512), BF16),
            vm((8, 8, 128, 128), F32),
            vm((8, 128, 512), BF16),
            vm((8, 128, 128), BF16),
            vm((8, 128, 128), BF16),
            vm((64, 2, 32, 128), BF16),
            vm((64, 32, 128), BF16),
            vm((128, 128), BF16),
            vm((128, 128), BF16),
            vm((4, 4, 4, 32, 128), F32),
            vm((4, 4, 4, 32, 128), BF16),
            vm((3, 4, 4, 16, 128), BF16),
            vm((3, 4, 4, 16, 128), BF16),
            vm((4, 4, 16, 128), F32),
            vm((4, 4, 16, 128), F32),
            vm((3, 4, 16, 128), BF16),
            vm((3, 4, 16, 128), BF16),
            vm((3, 4, 16, 128), BF16),
            vm((3, 4, 16, 128), BF16),
            vm((4, 32, 128), F32),
            vm((3, 32, 128), BF16),
            vm((3, 32, 128), BF16),
            vm((128, 4096), BF16),
            pltpu.SemaphoreType.DMA((23,)),
            pltpu.SemaphoreType.DMA((23,)),
            pltpu.SemaphoreType.DMA((8,)),
            pltpu.SemaphoreType.DMA((3,)),
        ],
        compiler_params=pltpu.CompilerParams(
            collective_id=0, has_side_effects=True, vmem_limit_bytes=60 * 1024 * 1024
        ),
        name="layer_backward",
    )(scale, weight, hidden[0], inner[0], read[0], step[0], decay[0], fwd[0], rev[0])
    return gi[None], gh[None], gw


def solution(mesh):
    in_specs = (
        P("dp", "ctx", None),
        P(("dp", "ctx"), None),
        P(("dp", "ctx")),
        P("dp", "ctx", None),
        P("dp", "ctx", None),
        P("dp", None, "ctx"),
        P("dp", None, "ctx"),
        P("dp", "ctx", None),
        P("dp", "ctx", None),
    )
    out_specs = (P("dp", "ctx", None), P("dp", "ctx", None), P(("dp", "ctx"), None))
    return jax.shard_map(shards, mesh=mesh, in_specs=in_specs, out_specs=out_specs, check_vma=False)
```

```python
import jax
import jax.numpy as jnp
from jax import lax
from jax.experimental import pallas as pl
from jax.experimental.pallas import tpu as pltpu
from jax.sharding import PartitionSpec as P

MESH = pl.DeviceIdType.MESH
F32 = jnp.float32
BF16 = jnp.bfloat16
HIGH = lax.Precision.HIGHEST
GROUP = ((0, 1), (3, 0), (1, 0), (3, 1), (1, 1), (2, 0), (2, 1))
ACROSS = ((0, 0), (3, 0), (0, 1), (1, 0), (3, 1), (1, 1), (2, 0), (2, 1))
ISSUE = tuple(
    (name[0], int(name[1])) for name in "f0 f1 f2 r0 f3 r1 f4 r2 f5 r3 f6 r4 r5 r6 r7".split()
)
EARLY = 7
ZPEERS = ((0, 1), (1, 0), (1, 1))
POSITIONS = 16384
(
    S_WA, S_WB, S_WC, S_WD, S_STEP, S_DECAY, S_READ, S_READ2, S_FWD, S_REV, S_WRITE, S_WRITE2, S_INNER, S_TOTAL,
    S_GW, S_GI, S_HT, S_WBX, S_A1, S_B1, S_A2, S_B2, S_X,
) = range(23)


def remote(src, dst, send_sem, recv_sem, device):
    copy = pltpu.make_async_remote_copy(
        src_ref=src, dst_ref=dst, send_sem=send_sem, recv_sem=recv_sem, device_id=device, device_id_type=MESH
    )
    copy.start()


def drain(ref, sem):
    pltpu.make_async_copy(ref, ref, sem).wait()


def dot(a, b, dims=((1,), (0,)), precision=None):
    return lax.dot_general(a, b, (dims, ((), ())), precision=precision, preferred_element_type=F32)


def body(
    scale_ref, weight_hbm, hidden_hbm, inner_hbm, read_hbm, step_hbm, decay_hbm, fwd_hbm, rev_hbm,
    gi_out, gh_out, gw_out,
    wraw, wnat, hid, fr, rr, br, ir, rd, st, dc, wr,
    row_c, row_e, col, ex_r, ex_l, ex_f, ex_b, fac, pf, qf, carry, run,
    r0, l0, rb, lb, tsend, trecv, es, ga, gi, gws, gwr,
    ht, hsib, wbs, wbr, gf, gb, ra1, rb1, acca, accb, ha, ra2, hb, rb2, accx, hx, rx, gh,
    ss, rs, rin, rrev, ls,
):
    dp, ctx = lax.axis_index("dp"), lax.axis_index("ctx")
    y, zl = dp // 2, dp % 2
    zh, x, k = ctx // 8, (ctx // 2) % 4, ctx % 2
    j = ctx % 8
    other = 1 - zh

    def at(dx, dk):
        return ((x + dx) % 4) * 2 + (k + dk) % 2

    def group(slot):
        return {"dp": dp, "ctx": zh * 8 + slot}

    def across(slot):
        return {"dp": dp, "ctx": other * 8 + slot}

    def xpeer(dx):
        return {"dp": dp, "ctx": zh * 8 + ((x + dx) % 4) * 2 + k}

    def ypeer(dy):
        return {"dp": ((y + dy) % 4) * 2 + zl, "ctx": ctx}

    def zpeer(dl, dh):
        return {"dp": y * 2 + (zl + dl) % 2, "ctx": ((zh + dh) % 2) * 8 + j}

    sibling = {"dp": dp, "ctx": zh * 8 + x * 2 + (1 - k)}

    wcopy = pltpu.make_async_copy(weight_hbm, wraw, ls.at[0])
    wcopy.start()
    hcopy = pltpu.make_async_copy(hidden_hbm, hid, ls.at[1])
    hcopy.start()

    barrier = pltpu.get_barrier_semaphore()
    peers = [group(at(*o)) for o in GROUP] + [across(at(*o)) for o in ACROSS]
    peers += [ypeer(d) for d in (1, 2, 3)] + [zpeer(1, 0), zpeer(1, 1)]
    for peer in peers:
        pl.semaphore_signal(barrier, inc=1, device_id=peer, device_id_type=MESH)
    pl.semaphore_wait(barrier, len(peers))

    own = dp * 8 + zh * 4 + x
    wcopy.wait()
    wnat[own, k] = (wraw[...].astype(F32) * scale_ref[0]).astype(BF16)

    for o in GROUP:
        t = at(*o)
        remote(step_hbm.at[pl.ds(pl.multiple_of(t * 8, 8), 8), :], st.at[j], ss.at[S_STEP], rs.at[S_STEP], group(t))
        remote(decay_hbm.at[pl.ds(pl.multiple_of(t * 8, 8), 8), :], dc.at[j], ss.at[S_DECAY], rs.at[S_DECAY], group(t))
    for dx in (1, 2, 3):
        remote(wnat.at[own, k], wnat.at[own, k], ss.at[S_WA], rs.at[S_WA], xpeer(dx))
    for dx in (1, 2, 3):
        remote(read_hbm, rd.at[x, k], ss.at[S_READ], rs.at[S_READ], xpeer(dx))
    own_rows = pl.ds(pl.multiple_of(j * 8, 8), 8)
    own_cols = pl.ds(pl.multiple_of(j * 512, 512), 512)
    pltpu.make_async_copy(step_hbm.at[own_rows, :], st.at[j], rs.at[S_STEP]).start()
    pltpu.make_async_copy(decay_hbm.at[own_rows, :], dc.at[j], rs.at[S_DECAY]).start()
    pltpu.make_async_copy(read_hbm, rd.at[x, k], rs.at[S_READ]).start()
    pltpu.make_async_copy(fwd_hbm.at[:, own_cols], fr.at[j], rs.at[S_FWD]).start()
    for strand, n in ISSUE:
        t = at(*(GROUP[n] if strand == "f" else ACROSS[n]))
        cols = pl.ds(pl.multiple_of(t * 512, 512), 512)
        if strand == "f":
            remote(fwd_hbm.at[:, cols], fr.at[j], ss.at[S_FWD], rs.at[S_FWD], group(t))
        else:
            remote(rev_hbm.at[:, cols], rr.at[7 - j], ss.at[S_REV], rrev.at[7 - j], across(t))
    pltpu.make_async_copy(inner_hbm.at[:, own_cols], ir.at[j], rin.at[j]).start()

    drain(wnat.at[pl.ds(0, 3), 0], rs.at[S_WA])
    four = pl.ds(dp * 8 + zh * 4, 4)
    for dl, dh in ZPEERS:
        remote(wnat.at[four, k], wnat.at[four, k], ss.at[S_WB], rs.at[S_WB], zpeer(dl, dh))

    drain(st, rs.at[S_STEP])
    drain(dc, rs.at[S_DECAY])
    rows = lax.broadcasted_iota(jnp.int32, (128, 128), 0)
    lanes = lax.broadcasted_iota(jnp.int32, (128, 128), 1)
    upper = lanes >= rows
    lower = lanes <= rows
    first_half = lanes < 64
    decay = dc[...].reshape(64, 128)
    cum = dot(decay, upper.astype(F32), precision=HIGH)
    excl = cum - decay
    log_step = jnp.log(st[...].reshape(64, 128))
    end = jnp.broadcast_to(cum[:, 127:128], (64, 128))
    c1 = cum - log_step
    c2 = excl + log_step
    kinds = (c1, c2, jnp.exp(end - c1), jnp.exp(c2), jnp.exp(cum), jnp.exp(end - excl))
    row_c[...] = cum.reshape(8, 8, 128)
    row_e[...] = excl.reshape(8, 8, 128)
    block_decay = jnp.exp(end)
    head_of = lax.broadcasted_iota(jnp.int32, (8, 512), 1) // 64
    pick = head_of == lax.broadcasted_iota(jnp.int32, (8, 512), 0)
    pad = jnp.zeros((80, 128), F32)
    for b in range(8):
        part = [kind[8 * b : 8 * b + 8] for kind in kinds]
        col[b] = jnp.transpose(jnp.concatenate(part + [pad], axis=0))
        wide = jnp.where(pick, jnp.broadcast_to(block_decay[8 * b : 8 * b + 8, 0:1], (8, 512)), 0.0)
        fac[b] = jnp.broadcast_to(jnp.sum(wide, axis=0, keepdims=True), (8, 512))

    drain(wnat.at[pl.ds(0, 12), 0], rs.at[S_WB])
    sixteen = pl.ds(y * 16, 16)
    for dy in (2, 1, 3):
        remote(wnat.at[sixteen, k], wnat.at[sixteen, k], ss.at[S_WC], rs.at[S_WC], ypeer(dy))

    def column(b, index):
        return jnp.broadcast_to(col[b, :, index : index + 1], (128, 128))

    def decay_step(b, _):
        for h in range(8):
            arg = jnp.where(upper, row_c[b, h : h + 1, :] - column(b, h), column(b, 8 + h) - row_e[b, h : h + 1, :])
            es[b, h] = jnp.exp(arg)
        return 0

    lax.fori_loop(0, 8, decay_step, 0)

    def spread_step(b, _):
        for n, spread in enumerate((ex_r, ex_l, ex_f, ex_b)):
            for p in range(4):
                index = 16 + 8 * n + 2 * p
                spread[b, :, 128 * p : 128 * p + 128] = jnp.where(first_half, column(b, index), column(b, index + 1))
        return 0

    lax.fori_loop(0, 8, spread_step, 0)

    drain(rd.at[:, 0], rs.at[S_READ])
    remote(rd.at[:, k], rd.at[:, k], ss.at[S_READ2], rs.at[S_READ2], sibling)

    hcopy.wait()
    for c in range(8):
        turned = jnp.transpose(hid[:, 512 * c : 512 * c + 512])
        ht[8 * c : 8 * c + 8] = turned.reshape(8, 2, 32, 128)

    drain(wnat.at[pl.ds(0, 48), 0], rs.at[S_WC])
    remote(wnat.at[:, k], wnat.at[:, k], ss.at[S_WD], rs.at[S_WD], sibling)
    remote(ht.at[:, 1 - k], hsib, ss.at[S_HT], rs.at[S_HT], sibling)

    drain(rd.at[:, 0], rs.at[S_READ2])
    drain(fr, rs.at[S_FWD])
    carry[...] = jnp.zeros_like(carry)
    run[...] = jnp.ones_like(run)

    def right_step(i, _):
        b = 7 - i
        pf[b] = run[...]
        run[...] = run[...] * fac[b]
        for p in range(4):
            sl = slice(128 * p, 128 * p + 128)
            scaled = (fr[b, :, sl].astype(F32) * ex_f[b, :, sl]).astype(BF16)
            part = dot(rd[b // 2, b % 2], scaled, ((0,), (0,)))
            old = carry[:, sl]
            r0[b, :, sl] = old
            carry[:, sl] = part + fac[b, 0:1, sl] * old
        return 0

    lax.fori_loop(0, 8, right_step, 0)

    drain(wnat.at[:, 0], rs.at[S_WD])
    write = jnp.zeros((128, 128), F32)
    for c in range(8):
        write += dot(hid[:, 512 * c : 512 * c + 512], wnat[8 * c : 8 * c + 8].reshape(512, 128))
    wr[x, k] = write.astype(BF16)

    @pl.when(zh == 1)
    def _():
        tsend[...] = carry[...].astype(BF16)

    for dx in (1, 2, 3):
        remote(wr.at[x, k], wr.at[x, k], ss.at[S_WRITE], rs.at[S_WRITE], xpeer(dx))
    def send_inner(offsets):
        for o in offsets:
            t = at(*o)
            cols = pl.ds(pl.multiple_of(t * 512, 512), 512)
            remote(inner_hbm.at[:, cols], ir.at[j], ss.at[S_INNER], rin.at[j], group(t))

    send_inner(GROUP[:EARLY])

    def arrival(i):
        q = i // 2
        return at((q * (q + 1) // 2) % 4, i % 2)

    flip = (rows + lanes == 127).astype(F32).astype(BF16)

    def back_step(i, _):
        b = 7 - arrival(i)
        drain(rr.at[0], rrev.at[b])
        for p in range(4):
            sl = slice(128 * p, 128 * p + 128)
            back = dot(flip, rr[b, :, sl])
            br[b, :, sl] = back.astype(BF16)
            l0[b, :, sl] = dot(rd[b // 2, b % 2], (back * ex_b[b, :, sl]).astype(BF16), ((0,), (0,)))
        return 0

    lax.fori_loop(0, 8, back_step, 0)
    carry[...] = jnp.zeros_like(carry)
    run[...] = jnp.ones_like(run)

    def left_step(b, _):
        qf[b] = run[...]
        run[...] = run[...] * fac[b]
        old = carry[...]
        carry[...] = l0[b] + fac[b, 0:1, :] * old
        l0[b] = old
        return 0

    lax.fori_loop(0, 8, left_step, 0)

    @pl.when(zh == 0)
    def _():
        tsend[...] = carry[...].astype(BF16)

    remote(tsend, trecv, ss.at[S_TOTAL], rs.at[S_TOTAL], across(j))
    send_inner(GROUP[EARLY:])

    drain(wr.at[pl.ds(0, 3), 0], rs.at[S_WRITE])
    remote(wr.at[:, k], wr.at[:, k], ss.at[S_WRITE2], rs.at[S_WRITE2], sibling)
    drain(wr.at[:, 0], rs.at[S_WRITE2])

    def stacked(b, sl):
        return jnp.concatenate([fr[b, :, sl], br[b, :, sl]], axis=0)

    def inner_grad_step(b, _):
        kern = dot(wr[b // 2, b % 2], rd[b // 2, b % 2], ((1,), (1,)))
        for p in range(4):
            sl = slice(128 * p, 128 * p + 128)
            mixes = []
            for h in (2 * p, 2 * p + 1):
                both = es[b, h] * kern
                mixes.append(
                    jnp.concatenate([jnp.where(upper, both, 0.0).astype(BF16), jnp.where(lower, both, 0.0).astype(BF16)], axis=1)
                )
            out = dot(jnp.concatenate(mixes, axis=0), stacked(b, sl))
            ga[b, :, sl] = jnp.where(first_half, out[:128], out[128:])
        return 0

    lax.fori_loop(0, 8, inner_grad_step, 0)

    half = first_half.astype(F32)
    mask_a = half.astype(BF16)
    mask_b = (1.0 - half).astype(BF16)

    drain(trecv, rs.at[S_TOTAL])
    low = (1 - zh).astype(F32)
    high = zh.astype(F32)

    def edge_step(b, _):
        far = trecv[...].astype(F32)
        rb[b] = (r0[b] + (pf[b, 0:1, :] * low) * far).astype(BF16)
        lb[b] = (l0[b] + (qf[b, 0:1, :] * high) * far).astype(BF16)
        return 0

    lax.fori_loop(0, 8, edge_step, 0)

    def write_grad_step(i, _):
        b = arrival(i)
        drain(ir.at[0], rin.at[b])
        mixed = jnp.zeros((128, 128), F32)
        for p in range(4):
            sl = slice(128 * p, 128 * p + 128)
            act = ir[b, :, sl]
            dots = dot(jnp.concatenate([act * mask_a, act * mask_b], axis=0), stacked(b, sl), ((1,), (1,)))
            for a in range(2):
                d = dots[128 * a : 128 * a + 128]
                mixed += es[b, 2 * p + a] * (jnp.where(upper, d[:, :128], 0.0) + jnp.where(lower, d[:, 128:], 0.0))
        act = ir[b].astype(F32)
        part = dot((act * ex_r[b]).astype(BF16), rb[b], ((1,), (1,)))
        part += dot((act * ex_l[b]).astype(BF16), lb[b], ((1,), (1,)))
        part = (dot(mixed.astype(BF16), rd[b // 2, b % 2]) + part).astype(BF16)
        gws[b] = part

        @pl.when(i == 0)
        def _():
            gwr[b] = part

        @pl.when(i > 0)
        def _():
            remote(gws.at[b], gwr.at[j], ss.at[S_GW], rs.at[S_GW], group(b))

        return 0

    lax.fori_loop(0, 8, write_grad_step, 0)

    def inner_edge_step(i, _):
        b = arrival(7 - i)
        write_b = wr[b // 2, b % 2]
        edge = ex_r[b] * dot(write_b, rb[b]) + ex_l[b] * dot(write_b, lb[b])
        gi[b] = (ga[b] + edge).astype(BF16)
        return 0

    lax.fori_loop(0, 8, inner_edge_step, 0)
    pltpu.make_async_copy(gi.at[j], gi_out.at[:, own_cols], rs.at[S_GI]).start()

    for o in GROUP[:3]:
        t = at(*o)
        remote(gi.at[t], gi_out.at[:, own_cols], ss.at[S_GI], rs.at[S_GI], group(t))
    drain(gwr.at[pl.ds(0, 7)], rs.at[S_GW])
    total = gwr[0].astype(F32)
    for b in range(1, 8):
        total += gwr[b].astype(F32)
    wb = total.astype(BF16)

    wbs[...] = wb
    remote(wbs, wbr, ss.at[S_WBX], rs.at[S_WBX], sibling)
    for o in GROUP[3:]:
        t = at(*o)
        remote(gi.at[t], gi_out.at[:, own_cols], ss.at[S_GI], rs.at[S_GI], group(t))

    drain(hsib, rs.at[S_HT])
    for yt in range(4):
        gf[yt] = dot(ht[16 * yt : 16 * yt + 16, k].reshape(512, 128), wb).reshape(4, 4, 32, 128)
    drain(wbr, rs.at[S_WBX])
    wbo = wbr[...]
    for dy in (2, 1, 3, 0):
        yt = (y + dy) % 4
        piece = gf[yt] + dot(hsib[pl.ds(yt * 16, 16)].reshape(512, 128), wbo).reshape(4, 4, 32, 128)
        gf[yt] = piece
        gb[yt] = piece.astype(BF16)
        if dy:
            remote(gb.at[yt, :, :, pl.ds(0, 16)], ra1.at[dy - 1], ss.at[S_A1], rs.at[S_A1], ypeer(dy))
    zown = zl * 2 + zh
    zts = [((zl + dl) % 2) * 2 + (zh + dh) % 2 for dl, dh in ZPEERS]
    for n, (dl, dh) in enumerate(ZPEERS):
        remote(gb.at[:, zts[n], :, pl.ds(16, 16)], rb1.at[n], ss.at[S_B1], rs.at[S_B1], zpeer(dl, dh))

    drain(ra1, rs.at[S_A1])
    acca[...] = gf[y, :, :, :16] + (ra1[0].astype(F32) + ra1[1].astype(F32) + ra1[2].astype(F32))
    for n, (dl, dh) in enumerate(ZPEERS):
        ha[n] = acca[zts[n]].astype(BF16)
        remote(ha.at[n], ra2.at[n], ss.at[S_A2], rs.at[S_A2], zpeer(dl, dh))
    drain(rb1, rs.at[S_B1])
    accb[...] = gf[:, zown, :, 16:] + (rb1[0].astype(F32) + rb1[1].astype(F32) + rb1[2].astype(F32))
    for dy in (2, 1, 3):
        hb[dy - 1] = accb[(y + dy) % 4].astype(BF16)
        remote(hb.at[dy - 1], rb2.at[dy - 1], ss.at[S_B2], rs.at[S_B2], ypeer(dy))
    for c in range(8):
        rows_c = wnat[8 * c : 8 * c + 8].reshape(512, 128)
        gh[:, 512 * c : 512 * c + 512] = dot(wb, rows_c, ((1,), (1,))).astype(BF16)
    ghcopy = pltpu.make_async_copy(gh, gh_out, ls.at[2])
    ghcopy.start()

    drain(ra2, rs.at[S_A2])
    accx[:, :16] = acca[zown] + (ra2[0].astype(F32) + ra2[1].astype(F32) + ra2[2].astype(F32))
    drain(rb2, rs.at[S_B2])
    accx[:, 16:] = accb[y] + (rb2[0].astype(F32) + rb2[1].astype(F32) + rb2[2].astype(F32))
    for dx in (1, 2, 3):
        hx[dx - 1] = accx[(x + dx) % 4].astype(BF16)
        remote(hx.at[dx - 1], rx.at[dx - 1], ss.at[S_X], rs.at[S_X], xpeer(dx))
    drain(rx, rs.at[S_X])
    gw_out[...] = (accx[x] + (rx[0].astype(F32) + rx[1].astype(F32) + rx[2].astype(F32))) * (1.0 / POSITIONS)

    drain(wnat.at[pl.ds(0, 3), 0], ss.at[S_WA])
    drain(wnat.at[pl.ds(0, 12), 0], ss.at[S_WB])
    drain(wnat.at[pl.ds(0, 48), 0], ss.at[S_WC])
    drain(wnat.at[:, 0], ss.at[S_WD])
    drain(st.at[pl.ds(0, 7)], ss.at[S_STEP])
    drain(dc.at[pl.ds(0, 7)], ss.at[S_DECAY])
    drain(rd.at[pl.ds(0, 3), 0], ss.at[S_READ])
    drain(rd.at[:, 0], ss.at[S_READ2])
    drain(hsib, ss.at[S_HT])
    drain(wbs, ss.at[S_WBX])
    drain(fr.at[pl.ds(0, 7)], ss.at[S_FWD])
    drain(rr, ss.at[S_REV])
    drain(wr.at[pl.ds(0, 3), 0], ss.at[S_WRITE])
    drain(wr.at[:, 0], ss.at[S_WRITE2])
    drain(ir.at[pl.ds(0, 7)], ss.at[S_INNER])
    drain(tsend, ss.at[S_TOTAL])
    drain(gws.at[pl.ds(0, 7)], ss.at[S_GW])
    drain(gi.at[pl.ds(0, 7)], ss.at[S_GI])
    drain(ra1, ss.at[S_A1])
    drain(rb1, ss.at[S_B1])
    drain(ha, ss.at[S_A2])
    drain(hb, ss.at[S_B2])
    drain(hx, ss.at[S_X])
    ghcopy.wait()
    drain(gi, rs.at[S_GI])


def results(a, b, c, a_out, b_out, c_out, sem):
    copies = [pltpu.make_async_copy(s, d, sem.at[n]) for n, (s, d) in enumerate(((a, a_out), (b, b_out), (c, c_out)))]
    for copy in copies:
        copy.start()
    for copy in copies:
        copy.wait()


def shards(hidden, weight, scale, inner, read, step, decay, fwd, rev):
    hbm = pl.BlockSpec(memory_space=pl.ANY)
    vm = pltpu.VMEM
    shapes = (
        jax.ShapeDtypeStruct((128, 4096), BF16),
        jax.ShapeDtypeStruct((128, 4096), BF16),
        jax.ShapeDtypeStruct((32, 128), F32),
    )
    arrays = (weight, hidden[0], inner[0], read[0], step[0], decay[0], fwd[0], rev[0])
    gi, gh, gw = pl.pallas_call(
        body,
        out_shape=shapes,
        in_specs=[pl.BlockSpec(memory_space=pltpu.SMEM)] + [hbm] * 8,
        out_specs=(hbm, hbm, pl.BlockSpec(memory_space=pltpu.VMEM)),
        scratch_shapes=[
            vm((32, 128), BF16),
            vm((64, 2, 32, 128), BF16),
            vm((128, 4096), BF16),
            vm((8, 128, 512), BF16),
            vm((8, 128, 512), BF16),
            vm((8, 128, 512), BF16),
            vm((8, 128, 512), BF16),
            vm((4, 2, 128, 128), BF16),
            vm((8, 8, 128), F32),
            vm((8, 8, 128), F32),
            vm((4, 2, 128, 128), BF16),
            vm((8, 8, 128), F32),
            vm((8, 8, 128), F32),
            vm((8, 128, 128), F32),
            vm((8, 128, 512), F32),
            vm((8, 128, 512), F32),
            vm((8, 128, 512), F32),
            vm((8, 128, 512), F32),
            vm((8, 8, 512), F32),
            vm((8, 8, 512), F32),
            vm((8, 8, 512), F32),
            vm((128, 512), F32),
            vm((8, 512), F32),
            vm((8, 128, 512), F32),
            vm((8, 128, 512), F32),
            vm((8, 128, 512), BF16),
            vm((8, 128, 512), BF16),
            vm((128, 512), BF16),
            vm((128, 512), BF16),
            vm((8, 8, 128, 128), F32),
            vm((8, 128, 512), F32),
            vm((8, 128, 512), BF16),
            vm((8, 128, 128), BF16),
            vm((8, 128, 128), BF16),
            vm((64, 2, 32, 128), BF16),
            vm((64, 32, 128), BF16),
            vm((128, 128), BF16),
            vm((128, 128), BF16),
            vm((4, 4, 4, 32, 128), F32),
            vm((4, 4, 4, 32, 128), BF16),
            vm((3, 4, 4, 16, 128), BF16),
            vm((3, 4, 4, 16, 128), BF16),
            vm((4, 4, 16, 128), F32),
            vm((4, 4, 16, 128), F32),
            vm((3, 4, 16, 128), BF16),
            vm((3, 4, 16, 128), BF16),
            vm((3, 4, 16, 128), BF16),
            vm((3, 4, 16, 128), BF16),
            vm((4, 32, 128), F32),
            vm((3, 32, 128), BF16),
            vm((3, 32, 128), BF16),
            vm((128, 4096), BF16),
            pltpu.SemaphoreType.DMA((23,)),
            pltpu.SemaphoreType.DMA((23,)),
            pltpu.SemaphoreType.DMA((8,)),
            pltpu.SemaphoreType.DMA((8,)),
            pltpu.SemaphoreType.DMA((3,)),
        ],
        compiler_params=pltpu.CompilerParams(
            collective_id=0, has_side_effects=True, vmem_limit_bytes=44 * 1024 * 1024
        ),
        name="layer_backward",
    )(scale, *[pltpu.with_memory_space_constraint(a, pltpu.HBM) for a in arrays])
    gi, gh, gw = pl.pallas_call(
        results,
        out_shape=shapes,
        in_specs=[hbm] * 3,
        out_specs=(pl.BlockSpec(memory_space=pltpu.HBM),) * 3,
        scratch_shapes=[pltpu.SemaphoreType.DMA((3,))],
        compiler_params=pltpu.CompilerParams(vmem_limit_bytes=1024 * 1024),
        name="results",
    )(gi, gh, gw)
    return gi[None], gh[None], gw


def solution(mesh):
    in_specs = (
        P("dp", "ctx", None),
        P(("dp", "ctx"), None),
        P(("dp", "ctx")),
        P("dp", "ctx", None),
        P("dp", "ctx", None),
        P("dp", None, "ctx"),
        P("dp", None, "ctx"),
        P("dp", "ctx", None),
        P("dp", "ctx", None),
    )
    out_specs = (P("dp", "ctx", None), P("dp", "ctx", None), P(("dp", "ctx"), None))
    return jax.shard_map(shards, mesh=mesh, in_specs=in_specs, out_specs=out_specs, check_vma=False)
```

```python
import jax
import jax.numpy as jnp
from jax import lax
from jax.experimental import pallas as pl
from jax.experimental.pallas import tpu as pltpu
from jax.sharding import PartitionSpec as P

MESH = pl.DeviceIdType.MESH
F32 = jnp.float32
BF16 = jnp.bfloat16
HIGH = lax.Precision.HIGHEST
GROUP = ((0, 1), (3, 0), (1, 0), (3, 1), (1, 1), (2, 0), (2, 1))
ACROSS = ((0, 0), (3, 0), (0, 1), (1, 0), (3, 1), (1, 1), (2, 0), (2, 1))
ISSUE = tuple(
    (name[0], int(name[1])) for name in "f0 f1 r0 f2 f3 r1 f4 r2 f5 r3 f6 r4 r5 r6 r7".split()
)
EARLY = 13
HEAD = 3
READY = 5
COLUMN = ((2, 0), (2, 1), (1, 0), (3, 0), (1, 1), (3, 1), (0, 1))
ZPEERS = ((0, 1), (1, 0), (1, 1))
POSITIONS = 16384
(
    S_WA, S_WC, S_WD, S_STEP, S_DECAY, S_READ, S_READ2, S_FWD, S_REV, S_WRITE, S_WRITE2, S_INNER, S_TOTAL,
    S_GW, S_GI, S_HT, S_WBX, S_Z, S_X,
) = range(19)


def remote(src, dst, send_sem, recv_sem, device):
    copy = pltpu.make_async_remote_copy(
        src_ref=src, dst_ref=dst, send_sem=send_sem, recv_sem=recv_sem, device_id=device, device_id_type=MESH
    )
    copy.start()


def drain(ref, sem):
    pltpu.make_async_copy(ref, ref, sem).wait()


def dot(a, b, dims=((1,), (0,)), precision=None):
    return lax.dot_general(a, b, (dims, ((), ())), precision=precision, preferred_element_type=F32)


def body(
    scale_ref, weight_hbm, hidden_hbm, inner_hbm, read_hbm, step_hbm, decay_hbm, fwd_hbm, rev_hbm,
    gi_out, gh_out, gw_out,
    wraw, wnat, hid, fr, rr, br, ir, rd, st, dc, wr,
    row_c, row_e, col, ex_r, ex_l, ex_f, ex_b, fac, pf, qf, carry, run,
    r0, l0, rb, lb, tsend, trecv, es, ga, gwa, gi, gws, gwr,
    ht, hall, wbs, wbr, accz, hz, rz, accx, hx, rx, gh,
    ss, rs, rin, rrev, ls,
):
    dp, ctx = lax.axis_index("dp"), lax.axis_index("ctx")
    y, zl = dp // 2, dp % 2
    zh, x, k = ctx // 8, (ctx // 2) % 4, ctx % 2
    j = ctx % 8
    other = 1 - zh

    def at(dx, dk):
        return ((x + dx) % 4) * 2 + (k + dk) % 2

    def group(slot):
        return {"dp": dp, "ctx": zh * 8 + slot}

    def across(slot):
        return {"dp": dp, "ctx": other * 8 + slot}

    def xpeer(dx):
        return {"dp": dp, "ctx": zh * 8 + ((x + dx) % 4) * 2 + k}

    def ypeer(dy):
        return {"dp": ((y + dy) % 4) * 2 + zl, "ctx": ctx}

    def zpeer(dl, dh):
        return {"dp": y * 2 + (zl + dl) % 2, "ctx": ((zh + dh) % 2) * 8 + j}

    def zxpeer(dl, dh, dx):
        return {"dp": y * 2 + (zl + dl) % 2, "ctx": ((zh + dh) % 2) * 8 + ((x + dx) % 4) * 2 + k}

    def column_peer(dy, dk):
        return {"dp": ((y + dy) % 4) * 2 + zl, "ctx": zh * 8 + x * 2 + (k + dk) % 2}

    sibling = {"dp": dp, "ctx": zh * 8 + x * 2 + (1 - k)}

    wcopy = pltpu.make_async_copy(weight_hbm, wraw, ls.at[0])
    wcopy.start()
    hcopy = pltpu.make_async_copy(hidden_hbm, hid, ls.at[1])
    hcopy.start()

    barrier = pltpu.get_barrier_semaphore()
    peers = [group(at(*o)) for o in GROUP] + [across(at(*o)) for o in ACROSS]
    peers += [column_peer(dy, dk) for dy in (1, 2, 3) for dk in range(2)]
    peers += [zxpeer(1, dh, dx) for dh in range(2) for dx in range(4)]
    for peer in peers:
        pl.semaphore_signal(barrier, inc=1, device_id=peer, device_id_type=MESH)
    pl.semaphore_wait(barrier, len(peers))

    own = dp * 8 + zh * 4 + x
    wcopy.wait()
    wnat[own, k] = (wraw[...].astype(F32) * scale_ref[0]).astype(BF16)

    for dl, dh in ((0, 1), (1, 0), (1, 1), (0, 0)):
        for dx in (2, 1, 3, 0):
            if (dl, dh, dx) != (0, 0, 0):
                remote(wnat.at[own, k], wnat.at[own, k], ss.at[S_WA], rs.at[S_WA], zxpeer(dl, dh, dx))
    for o in GROUP:
        t = at(*o)
        remote(step_hbm.at[pl.ds(pl.multiple_of(t * 8, 8), 8), :], st.at[j], ss.at[S_STEP], rs.at[S_STEP], group(t))
        remote(decay_hbm.at[pl.ds(pl.multiple_of(t * 8, 8), 8), :], dc.at[j], ss.at[S_DECAY], rs.at[S_DECAY], group(t))
    for dx in (1, 2, 3):
        remote(read_hbm, rd.at[x, k], ss.at[S_READ], rs.at[S_READ], xpeer(dx))
    own_rows = pl.ds(pl.multiple_of(j * 8, 8), 8)
    own_cols = pl.ds(pl.multiple_of(j * 512, 512), 512)
    pltpu.make_async_copy(step_hbm.at[own_rows, :], st.at[j], rs.at[S_STEP]).start()
    pltpu.make_async_copy(decay_hbm.at[own_rows, :], dc.at[j], rs.at[S_DECAY]).start()
    pltpu.make_async_copy(read_hbm, rd.at[x, k], rs.at[S_READ]).start()
    pltpu.make_async_copy(fwd_hbm.at[:, own_cols], fr.at[j], rs.at[S_FWD]).start()

    def issue(pieces):
        for strand, n in pieces:
            t = at(*(GROUP[n] if strand == "f" else ACROSS[n]))
            cols = pl.ds(pl.multiple_of(t * 512, 512), 512)
            if strand == "f":
                remote(fwd_hbm.at[:, cols], fr.at[j], ss.at[S_FWD], rs.at[S_FWD], group(t))
            else:
                remote(rev_hbm.at[:, cols], rr.at[7 - j], ss.at[S_REV], rrev.at[7 - j], across(t))

    issue(ISSUE[:EARLY])
    pltpu.make_async_copy(inner_hbm.at[:, own_cols], ir.at[j], rin.at[j]).start()

    drain(wnat.at[pl.ds(0, 15), 0], rs.at[S_WA])
    sixteen = pl.ds(y * 16, 16)
    for dy in (2, 1, 3):
        remote(wnat.at[sixteen, k], wnat.at[sixteen, k], ss.at[S_WC], rs.at[S_WC], ypeer(dy))

    drain(st, rs.at[S_STEP])
    drain(dc, rs.at[S_DECAY])
    rows = lax.broadcasted_iota(jnp.int32, (128, 128), 0)
    lanes = lax.broadcasted_iota(jnp.int32, (128, 128), 1)
    upper = lanes >= rows
    lower = lanes <= rows
    first_half = lanes < 64
    decay = dc[...].reshape(64, 128)
    cum = dot(decay, upper.astype(F32), precision=HIGH)
    excl = cum - decay
    log_step = jnp.log(st[...].reshape(64, 128))
    end = jnp.broadcast_to(cum[:, 127:128], (64, 128))
    c1 = cum - log_step
    c2 = excl + log_step
    kinds = (c1, c2, jnp.exp(end - c1), jnp.exp(c2), jnp.exp(cum), jnp.exp(end - excl))
    row_c[...] = cum.reshape(8, 8, 128)
    row_e[...] = excl.reshape(8, 8, 128)
    block_decay = jnp.exp(end)
    head_of = lax.broadcasted_iota(jnp.int32, (8, 512), 1) // 64
    pick = head_of == lax.broadcasted_iota(jnp.int32, (8, 512), 0)
    pad = jnp.zeros((80, 128), F32)
    for b in range(8):
        part = [kind[8 * b : 8 * b + 8] for kind in kinds]
        col[b] = jnp.transpose(jnp.concatenate(part + [pad], axis=0))
        wide = jnp.where(pick, jnp.broadcast_to(block_decay[8 * b : 8 * b + 8, 0:1], (8, 512)), 0.0)
        fac[b] = jnp.broadcast_to(jnp.sum(wide, axis=0, keepdims=True), (8, 512))

    def column(b, index):
        return jnp.broadcast_to(col[b, :, index : index + 1], (128, 128))

    def decay_step(b, _):
        for h in range(8):
            arg = jnp.where(upper, row_c[b, h : h + 1, :] - column(b, h), column(b, 8 + h) - row_e[b, h : h + 1, :])
            es[b, h] = jnp.exp(arg)
        return 0

    lax.fori_loop(0, 8, decay_step, 0)

    drain(wnat.at[pl.ds(0, 48), 0], rs.at[S_WC])
    remote(wnat.at[:, k], wnat.at[:, k], ss.at[S_WD], rs.at[S_WD], sibling)

    def spread_step(b, _):
        for n, spread in enumerate((ex_r, ex_l, ex_f, ex_b)):
            for p in range(4):
                index = 16 + 8 * n + 2 * p
                spread[b, :, 128 * p : 128 * p + 128] = jnp.where(first_half, column(b, index), column(b, index + 1))
        return 0

    lax.fori_loop(0, 8, spread_step, 0)

    drain(rd.at[:, 0], rs.at[S_READ])
    remote(rd.at[:, k], rd.at[:, k], ss.at[S_READ2], rs.at[S_READ2], sibling)

    hcopy.wait()
    for c in range(8):
        turned = jnp.transpose(hid[:, 512 * c : 512 * c + 512])
        ht[8 * c : 8 * c + 8] = turned.reshape(8, 2, 32, 128)

    for dy, dk in COLUMN:
        part = pl.ds(((y + dy) % 4) * 16, 16)
        remote(ht.at[part, (k + dk) % 2], hall.at[2 * dy + dk], ss.at[S_HT], rs.at[S_HT], column_peer(dy, dk))

    drain(wnat.at[:, 0], rs.at[S_WD])
    write = jnp.zeros((128, 128), F32)
    for c in range(8):
        write += dot(hid[:, 512 * c : 512 * c + 512], wnat[8 * c : 8 * c + 8].reshape(512, 128))
    wr[x, k] = write.astype(BF16)

    for dx in (1, 2, 3):
        remote(wr.at[x, k], wr.at[x, k], ss.at[S_WRITE], rs.at[S_WRITE], xpeer(dx))
    def send_inner(offsets):
        for o in offsets:
            t = at(*o)
            cols = pl.ds(pl.multiple_of(t * 512, 512), 512)
            remote(inner_hbm.at[:, cols], ir.at[j], ss.at[S_INNER], rin.at[j], group(t))

    issue(ISSUE[EARLY:])
    send_inner(GROUP)

    drain(rd.at[:, 0], rs.at[S_READ2])
    drain(fr, rs.at[S_FWD])
    carry[...] = jnp.zeros_like(carry)
    run[...] = jnp.ones_like(run)

    def right_step(i, _):
        b = 7 - i
        pf[b] = run[...]
        run[...] = run[...] * fac[b]
        for p in range(4):
            sl = slice(128 * p, 128 * p + 128)
            scaled = (fr[b, :, sl].astype(F32) * ex_f[b, :, sl]).astype(BF16)
            part = dot(rd[b // 2, b % 2], scaled, ((0,), (0,)))
            old = carry[:, sl]
            r0[b, :, sl] = old
            carry[:, sl] = part + fac[b, 0:1, sl] * old
        return 0

    lax.fori_loop(0, 8, right_step, 0)

    @pl.when(zh == 1)
    def _():
        tsend[...] = carry[...].astype(BF16)

    def back_arrival(i):
        q = i // 2
        return at((q * (q + 1) // 2) % 4, i % 2)

    def arrival(i):
        return back_arrival(i)

    flip = (rows + lanes == 127).astype(F32).astype(BF16)

    def back_step(i, _):
        b = 7 - back_arrival(i)
        drain(rr.at[0], rrev.at[b])
        for p in range(4):
            sl = slice(128 * p, 128 * p + 128)
            back = dot(flip, rr[b, :, sl])
            br[b, :, sl] = back.astype(BF16)
            l0[b, :, sl] = dot(rd[b // 2, b % 2], (back * ex_b[b, :, sl]).astype(BF16), ((0,), (0,)))
        return 0

    def stacked(b, sl):
        return jnp.concatenate([fr[b, :, sl], br[b, :, sl]], axis=0)

    def inner_grad_step(i, _):
        b = 7 - back_arrival(i)
        kern = dot(wr[b // 2, b % 2], rd[b // 2, b % 2], ((1,), (1,)))
        for p in range(4):
            sl = slice(128 * p, 128 * p + 128)
            mixes = []
            for h in (2 * p, 2 * p + 1):
                both = es[b, h] * kern
                mixes.append(
                    jnp.concatenate([jnp.where(upper, both, 0.0).astype(BF16), jnp.where(lower, both, 0.0).astype(BF16)], axis=1)
                )
            out = dot(jnp.concatenate(mixes, axis=0), stacked(b, sl))
            ga[b, :, sl] = jnp.where(first_half, out[:128], out[128:])
        return 0

    lax.fori_loop(0, 5, back_step, 0)
    drain(wr.at[pl.ds(0, 3), 0], rs.at[S_WRITE])
    remote(wr.at[:, k], wr.at[:, k], ss.at[S_WRITE2], rs.at[S_WRITE2], sibling)
    lax.fori_loop(5, 6, back_step, 0)
    drain(wr.at[:, 0], rs.at[S_WRITE2])
    lax.fori_loop(0, HEAD, inner_grad_step, 0)
    lax.fori_loop(6, 8, back_step, 0)
    carry[...] = jnp.zeros_like(carry)
    run[...] = jnp.ones_like(run)

    def left_step(b, _):
        qf[b] = run[...]
        run[...] = run[...] * fac[b]
        old = carry[...]
        carry[...] = l0[b] + fac[b, 0:1, :] * old
        l0[b] = old
        return 0

    lax.fori_loop(0, 8, left_step, 0)

    @pl.when(zh == 0)
    def _():
        tsend[...] = carry[...].astype(BF16)

    remote(tsend, trecv, ss.at[S_TOTAL], rs.at[S_TOTAL], across(j))

    lax.fori_loop(HEAD, 8, inner_grad_step, 0)

    half = first_half.astype(F32)
    mask_a = half.astype(BF16)
    mask_b = (1.0 - half).astype(BF16)

    def write_inside(i, _):
        b = arrival(i)
        drain(ir.at[0], rin.at[b])
        mixed = jnp.zeros((128, 128), F32)
        for p in range(4):
            sl = slice(128 * p, 128 * p + 128)
            act = ir[b, :, sl]
            dots = dot(jnp.concatenate([act * mask_a, act * mask_b], axis=0), stacked(b, sl), ((1,), (1,)))
            for a in range(2):
                d = dots[128 * a : 128 * a + 128]
                mixed += es[b, 2 * p + a] * (jnp.where(upper, d[:, :128], 0.0) + jnp.where(lower, d[:, 128:], 0.0))
        gwa[b] = dot(mixed.astype(BF16), rd[b // 2, b % 2])
        return 0

    def write_edge(i, _):
        b = arrival(i)
        act = ir[b].astype(F32)
        part = dot((act * ex_r[b]).astype(BF16), rb[b], ((1,), (1,)))
        part += dot((act * ex_l[b]).astype(BF16), lb[b], ((1,), (1,)))
        part = (gwa[b] + part).astype(BF16)
        gws[b] = part

        @pl.when(i == 0)
        def _():
            gwr[b] = part

        @pl.when(i > 0)
        def _():
            remote(gws.at[b], gwr.at[j], ss.at[S_GW], rs.at[S_GW], group(b))

        return 0

    def write_grad_step(i, _):
        write_inside(i, 0)
        return write_edge(i, 0)

    lax.fori_loop(0, READY, write_inside, 0)

    drain(trecv, rs.at[S_TOTAL])
    low = (1 - zh).astype(F32)
    high = zh.astype(F32)

    def edge_step(b, _):
        far = trecv[...].astype(F32)
        rb[b] = (r0[b] + (pf[b, 0:1, :] * low) * far).astype(BF16)
        lb[b] = (l0[b] + (qf[b, 0:1, :] * high) * far).astype(BF16)
        return 0

    lax.fori_loop(0, 8, edge_step, 0)

    lax.fori_loop(0, READY, write_edge, 0)
    lax.fori_loop(READY, 8, write_grad_step, 0)

    def inner_edge(b):
        write_b = wr[b // 2, b % 2]
        edge = ex_r[b] * dot(write_b, rb[b]) + ex_l[b] * dot(write_b, lb[b])
        gi[b] = (ga[b] + edge).astype(BF16)

        @pl.when(b != j)
        def _():
            remote(gi.at[b], gi_out.at[:, own_cols], ss.at[S_GI], rs.at[S_GI], group(b))

    def inner_edge_first(i, _):
        inner_edge(at(3 - 2 * (i // 2), i % 2))
        return 0

    def inner_edge_second(i, _):
        inner_edge(at(2 - 2 * (i // 2), i % 2))
        return 0

    lax.fori_loop(0, 4, inner_edge_first, 0)
    drain(gwr.at[pl.ds(0, 7)], rs.at[S_GW])
    total = gwr[0].astype(F32)
    for b in range(1, 8):
        total += gwr[b].astype(F32)
    wb = total.astype(BF16)

    wbs[...] = wb
    for dy, dk in COLUMN:
        remote(wbs, wbr.at[2 * dy + dk], ss.at[S_WBX], rs.at[S_WBX], column_peer(dy, dk))

    lax.fori_loop(0, 4, inner_edge_second, 0)
    pltpu.make_async_copy(gi.at[j], gi_out.at[:, own_cols], rs.at[S_GI]).start()

    drain(hall.at[pl.ds(0, 7)], rs.at[S_HT])
    piece = dot(ht[pl.ds(y * 16, 16), k].reshape(512, 128), wb)
    drain(wbr.at[pl.ds(0, 7)], rs.at[S_WBX])
    for dy, dk in COLUMN:
        piece += dot(hall[2 * dy + dk].reshape(512, 128), wbr[2 * dy + dk])
    accz[...] = piece.reshape(4, 4, 32, 128)
    for n, (dl, dh) in enumerate(ZPEERS):
        hz[n] = accz[((zl + dl) % 2) * 2 + (zh + dh) % 2].astype(BF16)
        remote(hz.at[n], rz.at[n], ss.at[S_Z], rs.at[S_Z], zpeer(dl, dh))
    for c in range(8):
        rows_c = wnat[8 * c : 8 * c + 8].reshape(512, 128)
        gh[:, 512 * c : 512 * c + 512] = dot(wb, rows_c, ((1,), (1,))).astype(BF16)
    ghcopy = pltpu.make_async_copy(gh, gh_out, ls.at[2])
    ghcopy.start()

    drain(rz, rs.at[S_Z])
    accx[...] = accz[zl * 2 + zh] + (rz[0].astype(F32) + rz[1].astype(F32) + rz[2].astype(F32))
    for dx in (1, 2, 3):
        hx[dx - 1] = accx[(x + dx) % 4].astype(BF16)
        remote(hx.at[dx - 1], rx.at[dx - 1], ss.at[S_X], rs.at[S_X], xpeer(dx))
    drain(rx, rs.at[S_X])
    gw_out[...] = (accx[x] + (rx[0].astype(F32) + rx[1].astype(F32) + rx[2].astype(F32))) * (1.0 / POSITIONS)

    drain(wnat.at[pl.ds(0, 15), 0], ss.at[S_WA])
    drain(wnat.at[pl.ds(0, 48), 0], ss.at[S_WC])
    drain(wnat.at[:, 0], ss.at[S_WD])
    drain(st.at[pl.ds(0, 7)], ss.at[S_STEP])
    drain(dc.at[pl.ds(0, 7)], ss.at[S_DECAY])
    drain(rd.at[pl.ds(0, 3), 0], ss.at[S_READ])
    drain(rd.at[:, 0], ss.at[S_READ2])
    drain(hall.at[pl.ds(0, 7)], ss.at[S_HT])
    drain(wbr.at[pl.ds(0, 7)], ss.at[S_WBX])
    drain(fr.at[pl.ds(0, 7)], ss.at[S_FWD])
    drain(rr, ss.at[S_REV])
    drain(wr.at[pl.ds(0, 3), 0], ss.at[S_WRITE])
    drain(wr.at[:, 0], ss.at[S_WRITE2])
    drain(ir.at[pl.ds(0, 7)], ss.at[S_INNER])
    drain(tsend, ss.at[S_TOTAL])
    drain(gws.at[pl.ds(0, 7)], ss.at[S_GW])
    drain(gi.at[pl.ds(0, 7)], ss.at[S_GI])
    drain(hz, ss.at[S_Z])
    drain(hx, ss.at[S_X])
    ghcopy.wait()
    drain(gi, rs.at[S_GI])


def results(a, b, c, a_out, b_out, c_out, sem):
    copies = [pltpu.make_async_copy(s, d, sem.at[n]) for n, (s, d) in enumerate(((a, a_out), (b, b_out), (c, c_out)))]
    for copy in copies:
        copy.start()
    for copy in copies:
        copy.wait()


def shards(hidden, weight, scale, inner, read, step, decay, fwd, rev):
    hbm = pl.BlockSpec(memory_space=pl.ANY)
    vm = pltpu.VMEM
    shapes = (
        jax.ShapeDtypeStruct((128, 4096), BF16),
        jax.ShapeDtypeStruct((128, 4096), BF16),
        jax.ShapeDtypeStruct((32, 128), F32),
    )
    arrays = (weight, hidden[0], inner[0], read[0], step[0], decay[0], fwd[0], rev[0])
    gi, gh, gw = pl.pallas_call(
        body,
        out_shape=shapes,
        in_specs=[pl.BlockSpec(memory_space=pltpu.SMEM)] + [hbm] * 8,
        out_specs=(hbm, hbm, pl.BlockSpec(memory_space=pltpu.VMEM)),
        scratch_shapes=[
            vm((32, 128), BF16),
            vm((64, 2, 32, 128), BF16),
            vm((128, 4096), BF16),
            vm((8, 128, 512), BF16),
            vm((8, 128, 512), BF16),
            vm((8, 128, 512), BF16),
            vm((8, 128, 512), BF16),
            vm((4, 2, 128, 128), BF16),
            vm((8, 8, 128), F32),
            vm((8, 8, 128), F32),
            vm((4, 2, 128, 128), BF16),
            vm((8, 8, 128), F32),
            vm((8, 8, 128), F32),
            vm((8, 128, 128), F32),
            vm((8, 128, 512), F32),
            vm((8, 128, 512), F32),
            vm((8, 128, 512), F32),
            vm((8, 128, 512), F32),
            vm((8, 8, 512), F32),
            vm((8, 8, 512), F32),
            vm((8, 8, 512), F32),
            vm((128, 512), F32),
            vm((8, 512), F32),
            vm((8, 128, 512), F32),
            vm((8, 128, 512), F32),
            vm((8, 128, 512), BF16),
            vm((8, 128, 512), BF16),
            vm((128, 512), BF16),
            vm((128, 512), BF16),
            vm((8, 8, 128, 128), F32),
            vm((8, 128, 512), F32),
            vm((8, 128, 128), F32),
            vm((8, 128, 512), BF16),
            vm((8, 128, 128), BF16),
            vm((8, 128, 128), BF16),
            vm((64, 2, 32, 128), BF16),
            vm((8, 16, 32, 128), BF16),
            vm((128, 128), BF16),
            vm((8, 128, 128), BF16),
            vm((4, 4, 32, 128), F32),
            vm((3, 4, 32, 128), BF16),
            vm((3, 4, 32, 128), BF16),
            vm((4, 32, 128), F32),
            vm((3, 32, 128), BF16),
            vm((3, 32, 128), BF16),
            vm((128, 4096), BF16),
            pltpu.SemaphoreType.DMA((19,)),
            pltpu.SemaphoreType.DMA((19,)),
            pltpu.SemaphoreType.DMA((8,)),
            pltpu.SemaphoreType.DMA((8,)),
            pltpu.SemaphoreType.DMA((3,)),
        ],
        compiler_params=pltpu.CompilerParams(
            collective_id=0, has_side_effects=True, vmem_limit_bytes=44 * 1024 * 1024
        ),
        name="layer_backward",
    )(scale, *[pltpu.with_memory_space_constraint(a, pltpu.HBM) for a in arrays])
    gi, gh, gw = pl.pallas_call(
        results,
        out_shape=shapes,
        in_specs=[hbm] * 3,
        out_specs=(pl.BlockSpec(memory_space=pltpu.HBM),) * 3,
        scratch_shapes=[pltpu.SemaphoreType.DMA((3,))],
        compiler_params=pltpu.CompilerParams(vmem_limit_bytes=1024 * 1024),
        name="results",
    )(gi, gh, gw)
    return gi[None], gh[None], gw


def solution(mesh):
    in_specs = (
        P("dp", "ctx", None),
        P(("dp", "ctx"), None),
        P(("dp", "ctx")),
        P("dp", "ctx", None),
        P("dp", "ctx", None),
        P("dp", None, "ctx"),
        P("dp", None, "ctx"),
        P("dp", "ctx", None),
        P("dp", "ctx", None),
    )
    out_specs = (P("dp", "ctx", None), P("dp", "ctx", None), P(("dp", "ctx"), None))
    return jax.shard_map(shards, mesh=mesh, in_specs=in_specs, out_specs=out_specs, check_vma=False)
```

```python
import jax
import jax.numpy as jnp
from jax import lax
from jax.experimental import pallas as pl
from jax.experimental.pallas import tpu as pltpu
from jax.sharding import PartitionSpec as P

MESH = pl.DeviceIdType.MESH
F32 = jnp.float32
BF16 = jnp.bfloat16
HIGH = lax.Precision.HIGHEST
GROUP = ((0, 1), (3, 0), (1, 0), (3, 1), (1, 1), (2, 0), (2, 1))
ACROSS = ((0, 0), (3, 0), (0, 1), (1, 0), (3, 1), (1, 1), (2, 0), (2, 1))
ISSUE = (
    ("f", 0), ("f", 1), ("r", 0), ("f", 2), ("f", 3),
    ("r", 1), ("f", 4), ("r", 2), ("f", 5), ("r", 3),
    ("f", 6), ("r", 4), ("r", 5), ("r", 6), ("r", 7),
)
EARLY = 13
HEAD = 3
READY = 5
COLUMN = ((2, 0), (2, 1), (1, 0), (3, 0), (1, 1), (3, 1), (0, 1))
ZPEERS = ((0, 1), (1, 0), (1, 1))
POSITIONS = 16384
(
    S_WA, S_WC, S_WD, S_STEP, S_DECAY, S_READ, S_READ2, S_FWD, S_REV, S_WRITE, S_WRITE2, S_INNER, S_TOTAL,
    S_GW, S_GI, S_HT, S_WBX, S_Z, S_X,
) = range(19)


def remote(src, dst, send_sem, recv_sem, device):
    copy = pltpu.make_async_remote_copy(
        src_ref=src, dst_ref=dst, send_sem=send_sem, recv_sem=recv_sem, device_id=device, device_id_type=MESH
    )
    copy.start()


def drain(ref, sem):
    pltpu.make_async_copy(ref, ref, sem).wait()


def dot(a, b, dims=((1,), (0,)), precision=None):
    return lax.dot_general(a, b, (dims, ((), ())), precision=precision, preferred_element_type=F32)


def body(
    scale_ref, weight_hbm, hidden_hbm, inner_hbm, read_hbm, step_hbm, decay_hbm, fwd_hbm, rev_hbm,
    gi_out, gh_out, gw_out,
    wraw, wnat, hid, fr, rr, br, ir, rd, st, dc, wr,
    row_c, row_e, col, ex_r, ex_l, ex_f, ex_b, fac, pf, qf, carry, run,
    r0, l0, rb, lb, tsend, trecv, es, ga, gwa, gi, gws, gwr,
    ht, hall, wbs, wbr, accz, hz, rz, accx, hx, rx, gh,
    ss, rs, rin, rrev, ls,
):
    dp, ctx = lax.axis_index("dp"), lax.axis_index("ctx")
    y, zl = dp // 2, dp % 2
    zh, x, k = ctx // 8, (ctx // 2) % 4, ctx % 2
    j = ctx % 8
    other = 1 - zh

    def at(dx, dk):
        return ((x + dx) % 4) * 2 + (k + dk) % 2

    def group(slot):
        return {"dp": dp, "ctx": zh * 8 + slot}

    def across(slot):
        return {"dp": dp, "ctx": other * 8 + slot}

    def xpeer(dx):
        return {"dp": dp, "ctx": zh * 8 + ((x + dx) % 4) * 2 + k}

    def ypeer(dy):
        return {"dp": ((y + dy) % 4) * 2 + zl, "ctx": ctx}

    def zpeer(dl, dh):
        return {"dp": y * 2 + (zl + dl) % 2, "ctx": ((zh + dh) % 2) * 8 + j}

    def zxpeer(dl, dh, dx):
        return {"dp": y * 2 + (zl + dl) % 2, "ctx": ((zh + dh) % 2) * 8 + ((x + dx) % 4) * 2 + k}

    def column_peer(dy, dk):
        return {"dp": ((y + dy) % 4) * 2 + zl, "ctx": zh * 8 + x * 2 + (k + dk) % 2}

    sibling = {"dp": dp, "ctx": zh * 8 + x * 2 + (1 - k)}

    wcopy = pltpu.make_async_copy(weight_hbm, wraw, ls.at[0])
    wcopy.start()
    hcopy = pltpu.make_async_copy(hidden_hbm, hid, ls.at[1])
    hcopy.start()

    barrier = pltpu.get_barrier_semaphore()
    peers = [group(at(*o)) for o in GROUP] + [across(at(*o)) for o in ACROSS]
    peers += [column_peer(dy, dk) for dy in (1, 2, 3) for dk in range(2)]
    peers += [zxpeer(1, dh, dx) for dh in range(2) for dx in range(4)]
    for peer in peers:
        pl.semaphore_signal(barrier, inc=1, device_id=peer, device_id_type=MESH)
    pl.semaphore_wait(barrier, len(peers))

    own = dp * 8 + zh * 4 + x
    wcopy.wait()
    wnat[own, k] = (wraw[...].astype(F32) * scale_ref[0]).astype(BF16)

    for dl, dh in ((0, 1), (1, 0), (1, 1), (0, 0)):
        for dx in (2, 1, 3, 0):
            if (dl, dh, dx) != (0, 0, 0):
                remote(wnat.at[own, k], wnat.at[own, k], ss.at[S_WA], rs.at[S_WA], zxpeer(dl, dh, dx))
    for o in GROUP:
        t = at(*o)
        remote(step_hbm.at[pl.ds(pl.multiple_of(t * 8, 8), 8), :], st.at[j], ss.at[S_STEP], rs.at[S_STEP], group(t))
        remote(decay_hbm.at[pl.ds(pl.multiple_of(t * 8, 8), 8), :], dc.at[j], ss.at[S_DECAY], rs.at[S_DECAY], group(t))
    for dx in (1, 2, 3):
        remote(read_hbm, rd.at[x, k], ss.at[S_READ], rs.at[S_READ], xpeer(dx))
    own_rows = pl.ds(pl.multiple_of(j * 8, 8), 8)
    own_cols = pl.ds(pl.multiple_of(j * 512, 512), 512)
    pltpu.make_async_copy(step_hbm.at[own_rows, :], st.at[j], rs.at[S_STEP]).start()
    pltpu.make_async_copy(decay_hbm.at[own_rows, :], dc.at[j], rs.at[S_DECAY]).start()
    pltpu.make_async_copy(read_hbm, rd.at[x, k], rs.at[S_READ]).start()
    pltpu.make_async_copy(fwd_hbm.at[:, own_cols], fr.at[j], rs.at[S_FWD]).start()

    def issue(pieces):
        for strand, n in pieces:
            t = at(*(GROUP[n] if strand == "f" else ACROSS[n]))
            cols = pl.ds(pl.multiple_of(t * 512, 512), 512)
            if strand == "f":
                remote(fwd_hbm.at[:, cols], fr.at[j], ss.at[S_FWD], rs.at[S_FWD], group(t))
            else:
                remote(rev_hbm.at[:, cols], rr.at[7 - j], ss.at[S_REV], rrev.at[7 - j], across(t))

    issue(ISSUE[:EARLY])
    pltpu.make_async_copy(inner_hbm.at[:, own_cols], ir.at[j], rin.at[j]).start()

    drain(wnat.at[pl.ds(0, 15), 0], rs.at[S_WA])
    sixteen = pl.ds(y * 16, 16)
    for dy in (2, 1, 3):
        remote(wnat.at[sixteen, k], wnat.at[sixteen, k], ss.at[S_WC], rs.at[S_WC], ypeer(dy))

    drain(st, rs.at[S_STEP])
    drain(dc, rs.at[S_DECAY])
    rows = lax.broadcasted_iota(jnp.int32, (128, 128), 0)
    lanes = lax.broadcasted_iota(jnp.int32, (128, 128), 1)
    upper = lanes >= rows
    lower = lanes <= rows
    first_half = lanes < 64
    decay = dc[...].reshape(64, 128)
    cum = dot(decay, upper.astype(F32), precision=HIGH)
    excl = cum - decay
    log_step = jnp.log(st[...].reshape(64, 128))
    end = jnp.broadcast_to(cum[:, 127:128], (64, 128))
    c1 = cum - log_step
    c2 = excl + log_step
    kinds = (c1, c2, jnp.exp(end - c1), jnp.exp(c2), jnp.exp(cum), jnp.exp(end - excl))
    row_c[...] = cum.reshape(8, 8, 128)
    row_e[...] = excl.reshape(8, 8, 128)
    block_decay = jnp.exp(end)
    head_of = lax.broadcasted_iota(jnp.int32, (8, 512), 1) // 64
    pick = head_of == lax.broadcasted_iota(jnp.int32, (8, 512), 0)
    pad = jnp.zeros((80, 128), F32)
    for b in range(8):
        part = [kind[8 * b : 8 * b + 8] for kind in kinds]
        col[b] = jnp.transpose(jnp.concatenate(part + [pad], axis=0))
        wide = jnp.where(pick, jnp.broadcast_to(block_decay[8 * b : 8 * b + 8, 0:1], (8, 512)), 0.0)
        fac[b] = jnp.broadcast_to(jnp.sum(wide, axis=0, keepdims=True), (8, 512))

    def column(b, index):
        return jnp.broadcast_to(col[b, :, index : index + 1], (128, 128))

    def decay_step(b, _):
        for h in range(8):
            arg = jnp.where(upper, row_c[b, h : h + 1, :] - column(b, h), column(b, 8 + h) - row_e[b, h : h + 1, :])
            es[b, h] = jnp.exp(arg)
        return 0

    lax.fori_loop(0, 8, decay_step, 0)

    drain(wnat.at[pl.ds(0, 48), 0], rs.at[S_WC])
    remote(wnat.at[:, k], wnat.at[:, k], ss.at[S_WD], rs.at[S_WD], sibling)

    def spread_step(b, _):
        for n, spread in enumerate((ex_r, ex_l, ex_f, ex_b)):
            for p in range(4):
                index = 16 + 8 * n + 2 * p
                spread[b, :, 128 * p : 128 * p + 128] = jnp.where(first_half, column(b, index), column(b, index + 1))
        return 0

    lax.fori_loop(0, 8, spread_step, 0)

    drain(rd.at[:, 0], rs.at[S_READ])
    remote(rd.at[:, k], rd.at[:, k], ss.at[S_READ2], rs.at[S_READ2], sibling)

    hcopy.wait()
    for c in range(8):
        turned = jnp.transpose(hid[:, 512 * c : 512 * c + 512])
        ht[8 * c : 8 * c + 8] = turned.reshape(8, 2, 32, 128)

    for dy, dk in COLUMN:
        part = pl.ds(((y + dy) % 4) * 16, 16)
        remote(ht.at[part, (k + dk) % 2], hall.at[2 * dy + dk], ss.at[S_HT], rs.at[S_HT], column_peer(dy, dk))

    drain(wnat.at[:, 0], rs.at[S_WD])
    write = jnp.zeros((128, 128), F32)
    for c in range(8):
        write += dot(hid[:, 512 * c : 512 * c + 512], wnat[8 * c : 8 * c + 8].reshape(512, 128))
    wr[x, k] = write.astype(BF16)

    for dx in (1, 2, 3):
        remote(wr.at[x, k], wr.at[x, k], ss.at[S_WRITE], rs.at[S_WRITE], xpeer(dx))
    def send_inner(offsets):
        for o in offsets:
            t = at(*o)
            cols = pl.ds(pl.multiple_of(t * 512, 512), 512)
            remote(inner_hbm.at[:, cols], ir.at[j], ss.at[S_INNER], rin.at[j], group(t))

    issue(ISSUE[EARLY:])
    send_inner(GROUP)

    drain(rd.at[:, 0], rs.at[S_READ2])
    drain(fr, rs.at[S_FWD])
    carry[...] = jnp.zeros_like(carry)
    run[...] = jnp.ones_like(run)

    def right_step(i, _):
        b = 7 - i
        pf[b] = run[...]
        run[...] = run[...] * fac[b]
        for p in range(4):
            sl = slice(128 * p, 128 * p + 128)
            scaled = (fr[b, :, sl].astype(F32) * ex_f[b, :, sl]).astype(BF16)
            part = dot(rd[b // 2, b % 2], scaled, ((0,), (0,)))
            old = carry[:, sl]
            r0[b, :, sl] = old
            carry[:, sl] = part + fac[b, 0:1, sl] * old
        return 0

    lax.fori_loop(0, 8, right_step, 0)

    @pl.when(zh == 1)
    def _():
        tsend[...] = carry[...].astype(BF16)

    def back_arrival(i):
        q = i // 2
        return at((q * (q + 1) // 2) % 4, i % 2)

    def arrival(i):
        return back_arrival(i)

    flip = (rows + lanes == 127).astype(F32).astype(BF16)

    def back_step(i, _):
        b = 7 - back_arrival(i)
        drain(rr.at[0], rrev.at[b])
        for p in range(4):
            sl = slice(128 * p, 128 * p + 128)
            back = dot(flip, rr[b, :, sl])
            br[b, :, sl] = back.astype(BF16)
            l0[b, :, sl] = dot(rd[b // 2, b % 2], (back * ex_b[b, :, sl]).astype(BF16), ((0,), (0,)))
        return 0

    def stacked(b, sl):
        return jnp.concatenate([fr[b, :, sl], br[b, :, sl]], axis=0)

    def inner_grad_step(i, _):
        b = 7 - back_arrival(i)
        kern = dot(wr[b // 2, b % 2], rd[b // 2, b % 2], ((1,), (1,)))
        for p in range(4):
            sl = slice(128 * p, 128 * p + 128)
            mixes = []
            for h in (2 * p, 2 * p + 1):
                both = es[b, h] * kern
                mixes.append(
                    jnp.concatenate([jnp.where(upper, both, 0.0).astype(BF16), jnp.where(lower, both, 0.0).astype(BF16)], axis=1)
                )
            out = dot(jnp.concatenate(mixes, axis=0), stacked(b, sl))
            ga[b, :, sl] = jnp.where(first_half, out[:128], out[128:])
        return 0

    lax.fori_loop(0, 5, back_step, 0)
    drain(wr.at[pl.ds(0, 3), 0], rs.at[S_WRITE])
    remote(wr.at[:, k], wr.at[:, k], ss.at[S_WRITE2], rs.at[S_WRITE2], sibling)
    lax.fori_loop(5, 6, back_step, 0)
    drain(wr.at[:, 0], rs.at[S_WRITE2])
    lax.fori_loop(0, HEAD, inner_grad_step, 0)
    lax.fori_loop(6, 8, back_step, 0)
    carry[...] = jnp.zeros_like(carry)
    run[...] = jnp.ones_like(run)

    def left_step(b, _):
        qf[b] = run[...]
        run[...] = run[...] * fac[b]
        old = carry[...]
        carry[...] = l0[b] + fac[b, 0:1, :] * old
        l0[b] = old
        return 0

    lax.fori_loop(0, 8, left_step, 0)

    @pl.when(zh == 0)
    def _():
        tsend[...] = carry[...].astype(BF16)

    remote(tsend, trecv, ss.at[S_TOTAL], rs.at[S_TOTAL], across(j))

    lax.fori_loop(HEAD, 8, inner_grad_step, 0)

    half = first_half.astype(F32)
    mask_a = half.astype(BF16)
    mask_b = (1.0 - half).astype(BF16)

    def write_inside(i, _):
        b = arrival(i)
        drain(ir.at[0], rin.at[b])
        mixed = jnp.zeros((128, 128), F32)
        for p in range(4):
            sl = slice(128 * p, 128 * p + 128)
            act = ir[b, :, sl]
            dots = dot(jnp.concatenate([act * mask_a, act * mask_b], axis=0), stacked(b, sl), ((1,), (1,)))
            for a in range(2):
                d = dots[128 * a : 128 * a + 128]
                mixed += es[b, 2 * p + a] * (jnp.where(upper, d[:, :128], 0.0) + jnp.where(lower, d[:, 128:], 0.0))
        gwa[b] = dot(mixed.astype(BF16), rd[b // 2, b % 2])
        return 0

    def write_edge(i, _):
        b = arrival(i)
        act = ir[b].astype(F32)
        part = dot((act * ex_r[b]).astype(BF16), rb[b], ((1,), (1,)))
        part += dot((act * ex_l[b]).astype(BF16), lb[b], ((1,), (1,)))
        part = (gwa[b] + part).astype(BF16)
        gws[b] = part

        @pl.when(i == 0)
        def _():
            gwr[b] = part

        @pl.when(i > 0)
        def _():
            remote(gws.at[b], gwr.at[j], ss.at[S_GW], rs.at[S_GW], group(b))

        return 0

    def write_grad_step(i, _):
        write_inside(i, 0)
        return write_edge(i, 0)

    lax.fori_loop(0, READY, write_inside, 0)

    drain(trecv, rs.at[S_TOTAL])
    low = (1 - zh).astype(F32)
    high = zh.astype(F32)

    def edge_step(b, _):
        far = trecv[...].astype(F32)
        rb[b] = (r0[b] + (pf[b, 0:1, :] * low) * far).astype(BF16)
        lb[b] = (l0[b] + (qf[b, 0:1, :] * high) * far).astype(BF16)
        return 0

    lax.fori_loop(0, 8, edge_step, 0)

    lax.fori_loop(0, READY, write_edge, 0)
    lax.fori_loop(READY, 8, write_grad_step, 0)

    def inner_edge(b):
        write_b = wr[b // 2, b % 2]
        edge = ex_r[b] * dot(write_b, rb[b]) + ex_l[b] * dot(write_b, lb[b])
        gi[b] = (ga[b] + edge).astype(BF16)

        @pl.when(b != j)
        def _():
            remote(gi.at[b], gi_out.at[:, own_cols], ss.at[S_GI], rs.at[S_GI], group(b))

    def inner_edge_first(i, _):
        inner_edge(at(3 - 2 * (i // 2), i % 2))
        return 0

    def inner_edge_second(i, _):
        inner_edge(at(2 - 2 * (i // 2), i % 2))
        return 0

    lax.fori_loop(0, 4, inner_edge_first, 0)
    drain(gwr.at[pl.ds(0, 7)], rs.at[S_GW])
    total = gwr[0].astype(F32)
    for b in range(1, 8):
        total += gwr[b].astype(F32)
    wb = total.astype(BF16)

    wbs[...] = wb
    for dy, dk in COLUMN:
        remote(wbs, wbr.at[2 * dy + dk], ss.at[S_WBX], rs.at[S_WBX], column_peer(dy, dk))

    lax.fori_loop(0, 4, inner_edge_second, 0)
    pltpu.make_async_copy(gi.at[j], gi_out.at[:, own_cols], rs.at[S_GI]).start()

    drain(hall.at[pl.ds(0, 7)], rs.at[S_HT])
    piece = dot(ht[pl.ds(y * 16, 16), k].reshape(512, 128), wb)
    drain(wbr.at[pl.ds(0, 7)], rs.at[S_WBX])
    for dy, dk in COLUMN:
        piece += dot(hall[2 * dy + dk].reshape(512, 128), wbr[2 * dy + dk])
    accz[...] = piece.reshape(4, 4, 32, 128)
    for n, (dl, dh) in enumerate(ZPEERS):
        hz[n] = accz[((zl + dl) % 2) * 2 + (zh + dh) % 2].astype(BF16)
        remote(hz.at[n], rz.at[n], ss.at[S_Z], rs.at[S_Z], zpeer(dl, dh))
    for c in range(8):
        rows_c = wnat[8 * c : 8 * c + 8].reshape(512, 128)
        gh[:, 512 * c : 512 * c + 512] = dot(wb, rows_c, ((1,), (1,))).astype(BF16)
    ghcopy = pltpu.make_async_copy(gh, gh_out, ls.at[2])
    ghcopy.start()

    drain(rz, rs.at[S_Z])
    accx[...] = accz[zl * 2 + zh] + (rz[0].astype(F32) + rz[1].astype(F32) + rz[2].astype(F32))
    for dx in (1, 2, 3):
        hx[dx - 1] = accx[(x + dx) % 4].astype(BF16)
        remote(hx.at[dx - 1], rx.at[dx - 1], ss.at[S_X], rs.at[S_X], xpeer(dx))
    drain(rx, rs.at[S_X])
    gw_out[...] = (accx[x] + (rx[0].astype(F32) + rx[1].astype(F32) + rx[2].astype(F32))) * (1.0 / POSITIONS)

    drain(wnat.at[pl.ds(0, 15), 0], ss.at[S_WA])
    drain(wnat.at[pl.ds(0, 48), 0], ss.at[S_WC])
    drain(wnat.at[:, 0], ss.at[S_WD])
    drain(st.at[pl.ds(0, 7)], ss.at[S_STEP])
    drain(dc.at[pl.ds(0, 7)], ss.at[S_DECAY])
    drain(rd.at[pl.ds(0, 3), 0], ss.at[S_READ])
    drain(rd.at[:, 0], ss.at[S_READ2])
    drain(hall.at[pl.ds(0, 7)], ss.at[S_HT])
    drain(wbr.at[pl.ds(0, 7)], ss.at[S_WBX])
    drain(fr.at[pl.ds(0, 7)], ss.at[S_FWD])
    drain(rr, ss.at[S_REV])
    drain(wr.at[pl.ds(0, 3), 0], ss.at[S_WRITE])
    drain(wr.at[:, 0], ss.at[S_WRITE2])
    drain(ir.at[pl.ds(0, 7)], ss.at[S_INNER])
    drain(tsend, ss.at[S_TOTAL])
    drain(gws.at[pl.ds(0, 7)], ss.at[S_GW])
    drain(gi.at[pl.ds(0, 7)], ss.at[S_GI])
    drain(hz, ss.at[S_Z])
    drain(hx, ss.at[S_X])
    ghcopy.wait()
    drain(gi, rs.at[S_GI])


def results(a, b, c, a_out, b_out, c_out, sem):
    copies = [pltpu.make_async_copy(s, d, sem.at[n]) for n, (s, d) in enumerate(((a, a_out), (b, b_out), (c, c_out)))]
    for copy in copies:
        copy.start()
    for copy in copies:
        copy.wait()


def shards(hidden, weight, scale, inner, read, step, decay, fwd, rev):
    hbm = pl.BlockSpec(memory_space=pl.ANY)
    vm = pltpu.VMEM
    shapes = (
        jax.ShapeDtypeStruct((128, 4096), BF16),
        jax.ShapeDtypeStruct((128, 4096), BF16),
        jax.ShapeDtypeStruct((32, 128), F32),
    )
    arrays = (weight, hidden[0], inner[0], read[0], step[0], decay[0], fwd[0], rev[0])
    gi, gh, gw = pl.pallas_call(
        body,
        out_shape=shapes,
        in_specs=[pl.BlockSpec(memory_space=pltpu.SMEM)] + [hbm] * 8,
        out_specs=(hbm, hbm, pl.BlockSpec(memory_space=pltpu.VMEM)),
        scratch_shapes=[
            vm((32, 128), BF16),
            vm((64, 2, 32, 128), BF16),
            vm((128, 4096), BF16),
            vm((8, 128, 512), BF16),
            vm((8, 128, 512), BF16),
            vm((8, 128, 512), BF16),
            vm((8, 128, 512), BF16),
            vm((4, 2, 128, 128), BF16),
            vm((8, 8, 128), F32),
            vm((8, 8, 128), F32),
            vm((4, 2, 128, 128), BF16),
            vm((8, 8, 128), F32),
            vm((8, 8, 128), F32),
            vm((8, 128, 128), F32),
            vm((8, 128, 512), F32),
            vm((8, 128, 512), F32),
            vm((8, 128, 512), F32),
            vm((8, 128, 512), F32),
            vm((8, 8, 512), F32),
            vm((8, 8, 512), F32),
            vm((8, 8, 512), F32),
            vm((128, 512), F32),
            vm((8, 512), F32),
            vm((8, 128, 512), F32),
            vm((8, 128, 512), F32),
            vm((8, 128, 512), BF16),
            vm((8, 128, 512), BF16),
            vm((128, 512), BF16),
            vm((128, 512), BF16),
            vm((8, 8, 128, 128), F32),
            vm((8, 128, 512), F32),
            vm((8, 128, 128), F32),
            vm((8, 128, 512), BF16),
            vm((8, 128, 128), BF16),
            vm((8, 128, 128), BF16),
            vm((64, 2, 32, 128), BF16),
            vm((8, 16, 32, 128), BF16),
            vm((128, 128), BF16),
            vm((8, 128, 128), BF16),
            vm((4, 4, 32, 128), F32),
            vm((3, 4, 32, 128), BF16),
            vm((3, 4, 32, 128), BF16),
            vm((4, 32, 128), F32),
            vm((3, 32, 128), BF16),
            vm((3, 32, 128), BF16),
            vm((128, 4096), BF16),
            pltpu.SemaphoreType.DMA((19,)),
            pltpu.SemaphoreType.DMA((19,)),
            pltpu.SemaphoreType.DMA((8,)),
            pltpu.SemaphoreType.DMA((8,)),
            pltpu.SemaphoreType.DMA((3,)),
        ],
        compiler_params=pltpu.CompilerParams(
            collective_id=0, has_side_effects=True, vmem_limit_bytes=44 * 1024 * 1024
        ),
        name="layer_backward",
    )(scale, *[pltpu.with_memory_space_constraint(a, pltpu.HBM) for a in arrays])
    gi, gh, gw = pl.pallas_call(
        results,
        out_shape=shapes,
        in_specs=[hbm] * 3,
        out_specs=(pl.BlockSpec(memory_space=pltpu.HBM),) * 3,
        scratch_shapes=[pltpu.SemaphoreType.DMA((3,))],
        compiler_params=pltpu.CompilerParams(vmem_limit_bytes=1024 * 1024),
        name="results",
    )(gi, gh, gw)
    return gi[None], gh[None], gw


def solution(mesh):
    in_specs = (
        P("dp", "ctx", None),
        P(("dp", "ctx"), None),
        P(("dp", "ctx")),
        P("dp", "ctx", None),
        P("dp", "ctx", None),
        P("dp", None, "ctx"),
        P("dp", None, "ctx"),
        P("dp", "ctx", None),
        P("dp", "ctx", None),
    )
    out_specs = (P("dp", "ctx", None), P("dp", "ctx", None), P(("dp", "ctx"), None))
    return jax.shard_map(shards, mesh=mesh, in_specs=in_specs, out_specs=out_specs, check_vma=False)
```

```python
import jax
import jax.numpy as jnp
from jax import lax
from jax.experimental import pallas as pl
from jax.experimental.pallas import tpu as pltpu
from jax.sharding import PartitionSpec as P

MESH = pl.DeviceIdType.MESH
F32 = jnp.float32
BF16 = jnp.bfloat16
HIGH = lax.Precision.HIGHEST
GROUP = ((0, 1), (3, 0), (1, 0), (3, 1), (1, 1), (2, 0), (2, 1))
ACROSS = ((0, 0), (3, 0), (0, 1), (1, 0), (3, 1), (1, 1), (2, 0), (2, 1))
ISSUE = (
    ("f", 0), ("f", 1), ("r", 0), ("f", 2), ("f", 3),
    ("r", 1), ("f", 4), ("r", 2), ("f", 5), ("r", 3),
    ("f", 6), ("r", 4), ("r", 5), ("r", 6), ("r", 7),
)
EARLY = 13
HEAD = 3
READY = 5
COLUMN = ((2, 0), (2, 1), (1, 0), (3, 0), (1, 1), (3, 1), (0, 1))
ZPEERS = ((0, 1), (1, 0), (1, 1))
POSITIONS = 16384
(
    S_WA, S_WC, S_WD, S_STEP, S_DECAY, S_READ, S_READ2, S_FWD, S_REV, S_WRITE, S_WRITE2, S_INNER, S_TOTAL,
    S_GW, S_GI, S_HT, S_WBX, S_Z, S_X,
) = range(19)


def remote(src, dst, send_sem, recv_sem, device):
    copy = pltpu.make_async_remote_copy(
        src_ref=src, dst_ref=dst, send_sem=send_sem, recv_sem=recv_sem, device_id=device, device_id_type=MESH
    )
    copy.start()


def drain(ref, sem):
    pltpu.make_async_copy(ref, ref, sem).wait()


def dot(a, b, dims=((1,), (0,)), precision=None):
    return lax.dot_general(a, b, (dims, ((), ())), precision=precision, preferred_element_type=F32)


def body(
    scale_ref, weight_hbm, hidden_hbm, inner_hbm, read_hbm, step_hbm, decay_hbm, fwd_hbm, rev_hbm,
    gi_out, gh_out, gw_out,
    wraw, wnat, hid, fr, rr, br, ir, rd, st, dc, wr,
    row_c, row_e, col, ex_r, ex_l, ex_f, ex_b, fac, pf, qf, carry, run,
    r0, l0, rb, lb, tsend, trecv, es, ga, gwa, gi, gws, gwr,
    ht, hall, wbs, wbr, accz, hz, rz, accx, hx, rx, gh,
    ss, rs, rin, rrev, ls,
):
    dp, ctx = lax.axis_index("dp"), lax.axis_index("ctx")
    y, zl = dp // 2, dp % 2
    zh, x, k = ctx // 8, (ctx // 2) % 4, ctx % 2
    j = ctx % 8
    other = 1 - zh

    def at(dx, dk):
        return ((x + dx) % 4) * 2 + (k + dk) % 2

    def group(slot):
        return {"dp": dp, "ctx": zh * 8 + slot}

    def across(slot):
        return {"dp": dp, "ctx": other * 8 + slot}

    def xpeer(dx):
        return {"dp": dp, "ctx": zh * 8 + ((x + dx) % 4) * 2 + k}

    def ypeer(dy):
        return {"dp": ((y + dy) % 4) * 2 + zl, "ctx": ctx}

    def zpeer(dl, dh):
        return {"dp": y * 2 + (zl + dl) % 2, "ctx": ((zh + dh) % 2) * 8 + j}

    def zxpeer(dl, dh, dx):
        return {"dp": y * 2 + (zl + dl) % 2, "ctx": ((zh + dh) % 2) * 8 + ((x + dx) % 4) * 2 + k}

    def column_peer(dy, dk):
        return {"dp": ((y + dy) % 4) * 2 + zl, "ctx": zh * 8 + x * 2 + (k + dk) % 2}

    sibling = {"dp": dp, "ctx": zh * 8 + x * 2 + (1 - k)}

    wcopy = pltpu.make_async_copy(weight_hbm, wraw, ls.at[0])
    wcopy.start()
    hcopy = pltpu.make_async_copy(hidden_hbm, hid, ls.at[1])
    hcopy.start()

    barrier = pltpu.get_barrier_semaphore()
    peers = [group(at(*o)) for o in GROUP] + [across(at(*o)) for o in ACROSS]
    peers += [column_peer(dy, dk) for dy in (1, 2, 3) for dk in range(2)]
    peers += [zxpeer(1, dh, dx) for dh in range(2) for dx in range(4)]
    for peer in peers:
        pl.semaphore_signal(barrier, inc=1, device_id=peer, device_id_type=MESH)
    pl.semaphore_wait(barrier, len(peers))

    own = dp * 8 + zh * 4 + x
    wcopy.wait()
    wnat[own, k] = (wraw[...].astype(F32) * scale_ref[0]).astype(BF16)

    for dl, dh in ((0, 1), (1, 0), (1, 1), (0, 0)):
        for dx in (2, 1, 3, 0):
            if (dl, dh, dx) != (0, 0, 0):
                remote(wnat.at[own, k], wnat.at[own, k], ss.at[S_WA], rs.at[S_WA], zxpeer(dl, dh, dx))
    for o in GROUP:
        t = at(*o)
        remote(step_hbm.at[pl.ds(pl.multiple_of(t * 8, 8), 8), :], st.at[j], ss.at[S_STEP], rs.at[S_STEP], group(t))
        remote(decay_hbm.at[pl.ds(pl.multiple_of(t * 8, 8), 8), :], dc.at[j], ss.at[S_DECAY], rs.at[S_DECAY], group(t))
    for dx in (1, 2, 3):
        remote(read_hbm, rd.at[x, k], ss.at[S_READ], rs.at[S_READ], xpeer(dx))
    own_rows = pl.ds(pl.multiple_of(j * 8, 8), 8)
    own_cols = pl.ds(pl.multiple_of(j * 512, 512), 512)
    pltpu.make_async_copy(step_hbm.at[own_rows, :], st.at[j], rs.at[S_STEP]).start()
    pltpu.make_async_copy(decay_hbm.at[own_rows, :], dc.at[j], rs.at[S_DECAY]).start()
    pltpu.make_async_copy(read_hbm, rd.at[x, k], rs.at[S_READ]).start()
    pltpu.make_async_copy(fwd_hbm.at[:, own_cols], fr.at[j], rs.at[S_FWD]).start()

    def issue(pieces):
        for strand, n in pieces:
            t = at(*(GROUP[n] if strand == "f" else ACROSS[n]))
            cols = pl.ds(pl.multiple_of(t * 512, 512), 512)
            if strand == "f":
                remote(fwd_hbm.at[:, cols], fr.at[j], ss.at[S_FWD], rs.at[S_FWD], group(t))
            else:
                remote(rev_hbm.at[:, cols], rr.at[7 - j], ss.at[S_REV], rrev.at[7 - j], across(t))

    issue(ISSUE[:EARLY])
    pltpu.make_async_copy(inner_hbm.at[:, own_cols], ir.at[j], rin.at[j]).start()

    drain(wnat.at[pl.ds(0, 15), 0], rs.at[S_WA])
    sixteen = pl.ds(y * 16, 16)
    for dy in (2, 1, 3):
        remote(wnat.at[sixteen, k], wnat.at[sixteen, k], ss.at[S_WC], rs.at[S_WC], ypeer(dy))

    drain(st, rs.at[S_STEP])
    drain(dc, rs.at[S_DECAY])
    rows = lax.broadcasted_iota(jnp.int32, (128, 128), 0)
    lanes = lax.broadcasted_iota(jnp.int32, (128, 128), 1)
    upper = lanes >= rows
    lower = lanes <= rows
    first_half = lanes < 64
    decay = dc[...].reshape(64, 128)
    cum = dot(decay, upper.astype(F32), precision=HIGH)
    excl = cum - decay
    log_step = jnp.log(st[...].reshape(64, 128))
    end = jnp.broadcast_to(cum[:, 127:128], (64, 128))
    c1 = cum - log_step
    c2 = excl + log_step
    kinds = (c1, c2, jnp.exp(end - c1), jnp.exp(c2), jnp.exp(cum), jnp.exp(end - excl))
    row_c[...] = cum.reshape(8, 8, 128)
    row_e[...] = excl.reshape(8, 8, 128)
    block_decay = jnp.exp(end)
    head_of = lax.broadcasted_iota(jnp.int32, (8, 512), 1) // 64
    pick = head_of == lax.broadcasted_iota(jnp.int32, (8, 512), 0)
    pad = jnp.zeros((80, 128), F32)
    for b in range(8):
        part = [kind[8 * b : 8 * b + 8] for kind in kinds]
        col[b] = jnp.transpose(jnp.concatenate(part + [pad], axis=0))
        wide = jnp.where(pick, jnp.broadcast_to(block_decay[8 * b : 8 * b + 8, 0:1], (8, 512)), 0.0)
        fac[b] = jnp.broadcast_to(jnp.sum(wide, axis=0, keepdims=True), (8, 512))

    def column(b, index):
        return jnp.broadcast_to(col[b, :, index : index + 1], (128, 128))

    def decay_step(b, _):
        for h in range(8):
            arg = jnp.where(upper, row_c[b, h : h + 1, :] - column(b, h), column(b, 8 + h) - row_e[b, h : h + 1, :])
            es[b, h] = jnp.exp(arg)
        return 0

    lax.fori_loop(0, 8, decay_step, 0)

    drain(wnat.at[pl.ds(0, 48), 0], rs.at[S_WC])
    remote(wnat.at[:, k], wnat.at[:, k], ss.at[S_WD], rs.at[S_WD], sibling)

    def spread_step(b, _):
        for n, spread in enumerate((ex_r, ex_l, ex_f, ex_b)):
            for p in range(4):
                index = 16 + 8 * n + 2 * p
                spread[b, :, 128 * p : 128 * p + 128] = jnp.where(first_half, column(b, index), column(b, index + 1))
        return 0

    lax.fori_loop(0, 8, spread_step, 0)

    drain(rd.at[:, 0], rs.at[S_READ])
    remote(rd.at[:, k], rd.at[:, k], ss.at[S_READ2], rs.at[S_READ2], sibling)

    hcopy.wait()
    for c in range(8):
        turned = jnp.transpose(hid[:, 512 * c : 512 * c + 512])
        ht[8 * c : 8 * c + 8] = turned.reshape(8, 2, 32, 128)

    for dy, dk in COLUMN:
        part = pl.ds(((y + dy) % 4) * 16, 16)
        remote(ht.at[part, (k + dk) % 2], hall.at[2 * dy + dk], ss.at[S_HT], rs.at[S_HT], column_peer(dy, dk))

    drain(wnat.at[:, 0], rs.at[S_WD])
    write = jnp.zeros((128, 128), F32)
    for c in range(8):
        write += dot(hid[:, 512 * c : 512 * c + 512], wnat[8 * c : 8 * c + 8].reshape(512, 128))
    wr[x, k] = write.astype(BF16)

    for dx in (1, 2, 3):
        remote(wr.at[x, k], wr.at[x, k], ss.at[S_WRITE], rs.at[S_WRITE], xpeer(dx))
    def send_inner(offsets):
        for o in offsets:
            t = at(*o)
            cols = pl.ds(pl.multiple_of(t * 512, 512), 512)
            remote(inner_hbm.at[:, cols], ir.at[j], ss.at[S_INNER], rin.at[j], group(t))

    issue(ISSUE[EARLY:])
    send_inner(GROUP)

    drain(rd.at[:, 0], rs.at[S_READ2])
    drain(fr, rs.at[S_FWD])
    carry[...] = jnp.zeros_like(carry)
    run[...] = jnp.ones_like(run)

    def right_step(i, _):
        b = 7 - i
        pf[b] = run[...]
        run[...] = run[...] * fac[b]
        for p in range(4):
            sl = slice(128 * p, 128 * p + 128)
            scaled = (fr[b, :, sl].astype(F32) * ex_f[b, :, sl]).astype(BF16)
            part = dot(rd[b // 2, b % 2], scaled, ((0,), (0,)))
            old = carry[:, sl]
            r0[b, :, sl] = old
            carry[:, sl] = part + fac[b, 0:1, sl] * old
        return 0

    lax.fori_loop(0, 8, right_step, 0)

    @pl.when(zh == 1)
    def _():
        tsend[...] = carry[...].astype(BF16)

    def back_arrival(i):
        q = i // 2
        return at((q * (q + 1) // 2) % 4, i % 2)

    def arrival(i):
        return back_arrival(i)

    flip = (rows + lanes == 127).astype(F32).astype(BF16)

    def back_step(i, _):
        b = 7 - back_arrival(i)
        drain(rr.at[0], rrev.at[b])
        for p in range(4):
            sl = slice(128 * p, 128 * p + 128)
            back = dot(flip, rr[b, :, sl])
            br[b, :, sl] = back.astype(BF16)
            l0[b, :, sl] = dot(rd[b // 2, b % 2], (back * ex_b[b, :, sl]).astype(BF16), ((0,), (0,)))
        return 0

    def stacked(b, sl):
        return jnp.concatenate([fr[b, :, sl], br[b, :, sl]], axis=0)

    def inner_grad_step(i, _):
        b = 7 - back_arrival(i)
        kern = dot(wr[b // 2, b % 2], rd[b // 2, b % 2], ((1,), (1,)))
        for p in range(4):
            sl = slice(128 * p, 128 * p + 128)
            mixes = []
            for h in (2 * p, 2 * p + 1):
                both = es[b, h] * kern
                mixes.append(
                    jnp.concatenate([jnp.where(upper, both, 0.0).astype(BF16), jnp.where(lower, both, 0.0).astype(BF16)], axis=1)
                )
            out = dot(jnp.concatenate(mixes, axis=0), stacked(b, sl))
            ga[b, :, sl] = jnp.where(first_half, out[:128], out[128:])
        return 0

    lax.fori_loop(0, 5, back_step, 0)
    drain(wr.at[pl.ds(0, 3), 0], rs.at[S_WRITE])
    remote(wr.at[:, k], wr.at[:, k], ss.at[S_WRITE2], rs.at[S_WRITE2], sibling)
    lax.fori_loop(5, 6, back_step, 0)
    drain(wr.at[:, 0], rs.at[S_WRITE2])
    lax.fori_loop(0, HEAD, inner_grad_step, 0)
    lax.fori_loop(6, 8, back_step, 0)
    carry[...] = jnp.zeros_like(carry)
    run[...] = jnp.ones_like(run)

    def left_step(b, _):
        qf[b] = run[...]
        run[...] = run[...] * fac[b]
        old = carry[...]
        carry[...] = l0[b] + fac[b, 0:1, :] * old
        l0[b] = old
        return 0

    lax.fori_loop(0, 8, left_step, 0)

    @pl.when(zh == 0)
    def _():
        tsend[...] = carry[...].astype(BF16)

    remote(tsend, trecv, ss.at[S_TOTAL], rs.at[S_TOTAL], across(j))

    lax.fori_loop(HEAD, 8, inner_grad_step, 0)

    half = first_half.astype(F32)
    mask_a = half.astype(BF16)
    mask_b = (1.0 - half).astype(BF16)

    def write_inside(i, _):
        b = arrival(i)
        drain(ir.at[0], rin.at[b])
        mixed = jnp.zeros((128, 128), F32)
        for p in range(4):
            sl = slice(128 * p, 128 * p + 128)
            act = ir[b, :, sl]
            dots = dot(jnp.concatenate([act * mask_a, act * mask_b], axis=0), stacked(b, sl), ((1,), (1,)))
            for a in range(2):
                d = dots[128 * a : 128 * a + 128]
                mixed += es[b, 2 * p + a] * (jnp.where(upper, d[:, :128], 0.0) + jnp.where(lower, d[:, 128:], 0.0))
        gwa[b] = dot(mixed.astype(BF16), rd[b // 2, b % 2])
        return 0

    def write_edge(i, _):
        b = arrival(i)
        act = ir[b].astype(F32)
        part = dot((act * ex_r[b]).astype(BF16), rb[b], ((1,), (1,)))
        part += dot((act * ex_l[b]).astype(BF16), lb[b], ((1,), (1,)))
        part = (gwa[b] + part).astype(BF16)
        gws[b] = part

        @pl.when(i == 0)
        def _():
            gwr[b] = part

        @pl.when(i > 0)
        def _():
            remote(gws.at[b], gwr.at[j], ss.at[S_GW], rs.at[S_GW], group(b))

        return 0

    def write_grad_step(i, _):
        write_inside(i, 0)
        return write_edge(i, 0)

    lax.fori_loop(0, READY, write_inside, 0)

    drain(trecv, rs.at[S_TOTAL])
    low = (1 - zh).astype(F32)
    high = zh.astype(F32)

    def edge_step(b, _):
        far = trecv[...].astype(F32)
        rb[b] = (r0[b] + (pf[b, 0:1, :] * low) * far).astype(BF16)
        lb[b] = (l0[b] + (qf[b, 0:1, :] * high) * far).astype(BF16)
        return 0

    lax.fori_loop(0, 8, edge_step, 0)

    lax.fori_loop(0, READY, write_edge, 0)
    lax.fori_loop(READY, 8, write_grad_step, 0)

    def inner_edge(b):
        write_b = wr[b // 2, b % 2]
        edge = ex_r[b] * dot(write_b, rb[b]) + ex_l[b] * dot(write_b, lb[b])
        gi[b] = (ga[b] + edge).astype(BF16)

        @pl.when(b != j)
        def _():
            remote(gi.at[b], gi_out.at[:, own_cols], ss.at[S_GI], rs.at[S_GI], group(b))

    def inner_edge_first(i, _):
        inner_edge(at(2 - i // 2, i % 2))
        return 0

    def inner_edge_second(i, _):
        inner_edge(at(3 - 3 * (i // 2), i % 2))
        return 0

    lax.fori_loop(0, 4, inner_edge_first, 0)
    drain(gwr.at[pl.ds(0, 7)], rs.at[S_GW])
    total = gwr[0].astype(F32)
    for b in range(1, 8):
        total += gwr[b].astype(F32)
    wb = total.astype(BF16)

    wbs[...] = wb
    for dy, dk in COLUMN:
        remote(wbs, wbr.at[2 * dy + dk], ss.at[S_WBX], rs.at[S_WBX], column_peer(dy, dk))

    lax.fori_loop(0, 4, inner_edge_second, 0)
    pltpu.make_async_copy(gi.at[j], gi_out.at[:, own_cols], rs.at[S_GI]).start()

    drain(hall.at[pl.ds(0, 7)], rs.at[S_HT])
    piece = dot(ht[pl.ds(y * 16, 16), k].reshape(512, 128), wb)
    drain(wbr.at[pl.ds(0, 7)], rs.at[S_WBX])
    for dy, dk in COLUMN:
        piece += dot(hall[2 * dy + dk].reshape(512, 128), wbr[2 * dy + dk])
    accz[...] = piece.reshape(4, 4, 32, 128)
    for n, (dl, dh) in enumerate(ZPEERS):
        hz[n] = accz[((zl + dl) % 2) * 2 + (zh + dh) % 2].astype(BF16)
        remote(hz.at[n], rz.at[n], ss.at[S_Z], rs.at[S_Z], zpeer(dl, dh))
    for c in range(8):
        rows_c = wnat[8 * c : 8 * c + 8].reshape(512, 128)
        gh[:, 512 * c : 512 * c + 512] = dot(wb, rows_c, ((1,), (1,))).astype(BF16)
    ghcopy = pltpu.make_async_copy(gh, gh_out, ls.at[2])
    ghcopy.start()

    drain(rz, rs.at[S_Z])
    accx[...] = accz[zl * 2 + zh] + (rz[0].astype(F32) + rz[1].astype(F32) + rz[2].astype(F32))
    for dx in (1, 2, 3):
        hx[dx - 1] = accx[(x + dx) % 4].astype(BF16)
        remote(hx.at[dx - 1], rx.at[dx - 1], ss.at[S_X], rs.at[S_X], xpeer(dx))
    drain(rx, rs.at[S_X])
    gw_out[...] = (accx[x] + (rx[0].astype(F32) + rx[1].astype(F32) + rx[2].astype(F32))) * (1.0 / POSITIONS)

    drain(wnat.at[pl.ds(0, 15), 0], ss.at[S_WA])
    drain(wnat.at[pl.ds(0, 48), 0], ss.at[S_WC])
    drain(wnat.at[:, 0], ss.at[S_WD])
    drain(st.at[pl.ds(0, 7)], ss.at[S_STEP])
    drain(dc.at[pl.ds(0, 7)], ss.at[S_DECAY])
    drain(rd.at[pl.ds(0, 3), 0], ss.at[S_READ])
    drain(rd.at[:, 0], ss.at[S_READ2])
    drain(hall.at[pl.ds(0, 7)], ss.at[S_HT])
    drain(wbr.at[pl.ds(0, 7)], ss.at[S_WBX])
    drain(fr.at[pl.ds(0, 7)], ss.at[S_FWD])
    drain(rr, ss.at[S_REV])
    drain(wr.at[pl.ds(0, 3), 0], ss.at[S_WRITE])
    drain(wr.at[:, 0], ss.at[S_WRITE2])
    drain(ir.at[pl.ds(0, 7)], ss.at[S_INNER])
    drain(tsend, ss.at[S_TOTAL])
    drain(gws.at[pl.ds(0, 7)], ss.at[S_GW])
    drain(gi.at[pl.ds(0, 7)], ss.at[S_GI])
    drain(hz, ss.at[S_Z])
    drain(hx, ss.at[S_X])
    ghcopy.wait()
    drain(gi, rs.at[S_GI])


def results(a, b, c, a_out, b_out, c_out, sem):
    copies = [pltpu.make_async_copy(s, d, sem.at[n]) for n, (s, d) in enumerate(((a, a_out), (b, b_out), (c, c_out)))]
    for copy in copies:
        copy.start()
    for copy in copies:
        copy.wait()


def shards(hidden, weight, scale, inner, read, step, decay, fwd, rev):
    hbm = pl.BlockSpec(memory_space=pl.ANY)
    vm = pltpu.VMEM
    shapes = (
        jax.ShapeDtypeStruct((128, 4096), BF16),
        jax.ShapeDtypeStruct((128, 4096), BF16),
        jax.ShapeDtypeStruct((32, 128), F32),
    )
    arrays = (weight, hidden[0], inner[0], read[0], step[0], decay[0], fwd[0], rev[0])
    gi, gh, gw = pl.pallas_call(
        body,
        out_shape=shapes,
        in_specs=[pl.BlockSpec(memory_space=pltpu.SMEM)] + [hbm] * 8,
        out_specs=(hbm, hbm, pl.BlockSpec(memory_space=pltpu.VMEM)),
        scratch_shapes=[
            vm((32, 128), BF16),
            vm((64, 2, 32, 128), BF16),
            vm((128, 4096), BF16),
            vm((8, 128, 512), BF16),
            vm((8, 128, 512), BF16),
            vm((8, 128, 512), BF16),
            vm((8, 128, 512), BF16),
            vm((4, 2, 128, 128), BF16),
            vm((8, 8, 128), F32),
            vm((8, 8, 128), F32),
            vm((4, 2, 128, 128), BF16),
            vm((8, 8, 128), F32),
            vm((8, 8, 128), F32),
            vm((8, 128, 128), F32),
            vm((8, 128, 512), F32),
            vm((8, 128, 512), F32),
            vm((8, 128, 512), F32),
            vm((8, 128, 512), F32),
            vm((8, 8, 512), F32),
            vm((8, 8, 512), F32),
            vm((8, 8, 512), F32),
            vm((128, 512), F32),
            vm((8, 512), F32),
            vm((8, 128, 512), F32),
            vm((8, 128, 512), F32),
            vm((8, 128, 512), BF16),
            vm((8, 128, 512), BF16),
            vm((128, 512), BF16),
            vm((128, 512), BF16),
            vm((8, 8, 128, 128), F32),
            vm((8, 128, 512), F32),
            vm((8, 128, 128), F32),
            vm((8, 128, 512), BF16),
            vm((8, 128, 128), BF16),
            vm((8, 128, 128), BF16),
            vm((64, 2, 32, 128), BF16),
            vm((8, 16, 32, 128), BF16),
            vm((128, 128), BF16),
            vm((8, 128, 128), BF16),
            vm((4, 4, 32, 128), F32),
            vm((3, 4, 32, 128), BF16),
            vm((3, 4, 32, 128), BF16),
            vm((4, 32, 128), F32),
            vm((3, 32, 128), BF16),
            vm((3, 32, 128), BF16),
            vm((128, 4096), BF16),
            pltpu.SemaphoreType.DMA((19,)),
            pltpu.SemaphoreType.DMA((19,)),
            pltpu.SemaphoreType.DMA((8,)),
            pltpu.SemaphoreType.DMA((8,)),
            pltpu.SemaphoreType.DMA((3,)),
        ],
        compiler_params=pltpu.CompilerParams(
            collective_id=0, has_side_effects=True, vmem_limit_bytes=44 * 1024 * 1024
        ),
        name="layer_backward",
    )(scale, *[pltpu.with_memory_space_constraint(a, pltpu.HBM) for a in arrays])
    gi, gh, gw = pl.pallas_call(
        results,
        out_shape=shapes,
        in_specs=[hbm] * 3,
        out_specs=(pl.BlockSpec(memory_space=pltpu.HBM),) * 3,
        scratch_shapes=[pltpu.SemaphoreType.DMA((3,))],
        compiler_params=pltpu.CompilerParams(vmem_limit_bytes=1024 * 1024),
        name="results",
    )(gi, gh, gw)
    return gi[None], gh[None], gw


def solution(mesh):
    in_specs = (
        P("dp", "ctx", None),
        P(("dp", "ctx"), None),
        P(("dp", "ctx")),
        P("dp", "ctx", None),
        P("dp", "ctx", None),
        P("dp", None, "ctx"),
        P("dp", None, "ctx"),
        P("dp", "ctx", None),
        P("dp", "ctx", None),
    )
    out_specs = (P("dp", "ctx", None), P("dp", "ctx", None), P(("dp", "ctx"), None))
    return jax.shard_map(shards, mesh=mesh, in_specs=in_specs, out_specs=out_specs, check_vma=False)
```
